32 devices in a mesh: samp: 4 (over y, x), var: 8 (over z, core).
Axes of the slice: x: 2, y: 2, z: 4, core: 2. Of those that a mesh axis runs over, the one named last changes fastest.
Arguments:
- observed: bfloat16 [1024, 32768], P('samp', 'var'), may hold values from -6 to 6
- blocks: float32 [256, 2, 128, 128], P('var'), may hold values from -6 to 6
- diagonal: float32 [32768], P('var'), may hold values from 1 to 4
- pattern: int32 [256, 2], P('var'), may hold values from 0 to 255, as said below
Outputs:
- new_blocks: float32 [256, 2, 128, 128], P('var')
- new_diagonal: float32 [32768], P('var')
- objective: float32 [2], replicated
The draws below stay inside these ranges and needn't reach their ends.
Inputs may be any that keep to these rules, and one draw needn't show every extreme that they name: pattern[c, 0] and pattern[c, 1] are two different row-block indices, one of them equal to c. For each index v of var, among its block columns c = v * 32 to v * 32 + 31, for every u, at most 4 of the entries that differ from c name row blocks in the range u * 32 to u * 32 + 31, and for some u exactly 4 do.
All inputs are finite; a program needn't handle non-finite values.
Results may differ from the reference program's by a relative error of at most 0.0049.
Values may be sent and summed in bfloat16 or wider, within the bound.
A program may use at most 128 MiB of HBM per device.

```python
import math
import jax
import jax.numpy as jnp
from jax import lax

BW = 128
CPD = 32
STEPS = 2
NBC = 256
P_SIZE = 32768
SAMPLES = 1024
CAP = 4
N_VAR = 8


def draw_pattern(key, part):
    first_draw = jax.random.randint(jax.random.fold_in(key, 11), (N_VAR,), 0, N_VAR)
    second_draw = jax.random.randint(jax.random.fold_in(key, 12), (N_VAR,), 0, N_VAR)
    reorder_permutation = jax.random.permutation(jax.random.fold_in(key, 13), N_VAR)
    hot_owner = reorder_permutation[first_draw * second_draw // N_VAR]
    offset = jax.random.randint(jax.random.fold_in(key, 14), (N_VAR, 1), 0, N_VAR - 1)
    position = jnp.arange(CPD, dtype=jnp.int32)[None, :]
    spread = (hot_owner[:, None] + 1 + (position - CAP + offset) % (N_VAR - 1)) % N_VAR
    owners = jnp.where(position < CAP, hot_owner[:, None], spread)
    scores = jax.random.randint(jax.random.fold_in(key, 15), (N_VAR, CPD), 0, 1024) * CPD + position
    column_order = jnp.argsort(scores, axis=1)
    owners = jnp.take_along_axis(owners, column_order, axis=1)
    resident_index = jax.random.randint(jax.random.fold_in(key, 16), (N_VAR, CPD), 0, CPD)
    devices = jnp.arange(N_VAR, dtype=jnp.int32)[:, None]
    own_column = devices * CPD + position
    row_block = owners * CPD + resident_index
    row_block = jnp.where(row_block == own_column, owners * CPD + (resident_index + 1) % CPD, row_block)
    slot_flip = jax.random.randint(jax.random.fold_in(key, 17), (N_VAR, CPD), 0, 2)
    paired = jnp.where((slot_flip == 0)[:, :, None], jnp.stack([own_column, row_block], -1), jnp.stack([row_block, own_column], -1))
    return paired.reshape(NBC, 2).astype(jnp.int32)


def levels(own_key, shape, split, smallest, top_value):
    gain, own = 1.0, jax.random.fold_in(own_key, 6)
    for axis_at, blocks in split:
        draws = jnp.exp(jax.random.uniform(jax.random.fold_in(own, axis_at), (blocks,), jnp.float32, smallest / len(split), top_value / len(split)))
        gain = gain * jnp.repeat(draws, shape[axis_at] // blocks).reshape([-1 if axis == axis_at else 1 for axis in range(len(shape))])
    return gain


def bell_draw(stream_key, dims, scale, most, cuts=(), kind=jnp.bfloat16):
    array = scale * jax.random.normal(stream_key, dims, jnp.float32)
    if cuts:
        array = array * levels(stream_key, dims, cuts, -0.22, 0.18)
    return jnp.clip(array, -most, most).astype(kind)


def setup_inputs(seed: int = 0) -> dict:
    seeds = jax.random.split(jax.random.key(seed), 5)
    observed = bell_draw(seeds[0], (SAMPLES, P_SIZE), 1.0, 6.0, ((0, 4), (1, 8)))
    blocks = bell_draw(seeds[1], (NBC, 2, BW, BW), 1.0, 6.0, ((0, 8),), jnp.float32)
    diagonal = jnp.clip(jnp.exp(math.log(4.0) - 1.3862944 * jax.random.uniform(seeds[2], (P_SIZE,), jnp.float32) ** levels(seeds[2], (P_SIZE,), ((0, 8),), -0.2, 0.2)), 1.0, 4.0)
    pattern = draw_pattern(jax.random.fold_in(seeds[4], 71), 0)
    return {"observed": observed, "blocks": blocks, "diagonal": diagonal, "pattern": pattern}


step_length = 0.5
penalty = 0.5

def shrink(moved, level):
    return jnp.sign(moved) * jnp.maximum(jnp.abs(moved) - level, 0.0)

def reference(observed, blocks, diagonal, pattern):
    block_count = blocks.shape[0]
    block_width = blocks.shape[2]
    sample_count = observed.shape[0]
    matrix_order = block_count * block_width
    group_size = math.gcd(block_count, 64)
    group_count = block_count // group_size
    column_tiles = observed.reshape(sample_count, block_count, block_width)
    columns = jnp.arange(block_count, dtype=jnp.int32)
    on_diag = pattern == columns[:, None]
    diag_mask = jnp.eye(block_width, dtype=bool)
    element_mask = on_diag[:, :, None, None] & diag_mask
    stored = jnp.where(element_mask, jnp.float32(0.0), blocks)
    diag_values = diagonal.reshape(block_count, block_width)

    def column_group(inputs):
        pattern_group, block_group, value_group, flag_group = inputs
        picked = jnp.take(column_tiles, pattern_group.reshape(-1), axis=1)
        picked = picked.reshape(sample_count, group_size, 2, block_width).astype(jnp.float32)
        full_blocks = jnp.where(flag_group[:, :, None, None] & diag_mask, value_group[:, None, None, :], block_group)
        rounded = lax.optimization_barrier(full_blocks.astype(jnp.bfloat16)).astype(jnp.float32)
        product = jnp.einsum('sgkb,gkbn->sgn', picked, rounded, precision=lax.Precision.HIGHEST)
        squares = jnp.sum(product * product)
        lower_precision_product = lax.optimization_barrier(product.astype(jnp.bfloat16)).astype(jnp.float32)
        gradient = jnp.einsum('sgkb,sgn->gkbn', picked, lower_precision_product, precision=lax.Precision.HIGHEST)
        return (gradient, squares)
    objectives = []
    for iteration in range(STEPS):
        gradient, squares = lax.map(column_group, (pattern.reshape(group_count, group_size, 2), stored.reshape(group_count, group_size, 2, block_width, block_width), diag_values.reshape(group_count, group_size, block_width), on_diag.reshape(group_count, group_size, 2)))
        gradient = gradient.reshape(block_count, 2, block_width, block_width) / sample_count
        total = -jnp.sum(jnp.log(diag_values)) + jnp.sum(squares) / (2.0 * sample_count) + penalty * jnp.sum(jnp.abs(stored))
        objectives.append(total / matrix_order)
        moved = stored - step_length * gradient
        stored = jnp.where(element_mask, jnp.float32(0.0), shrink(moved, step_length * penalty))
        along = lax.optimization_barrier(jnp.sum(jnp.where(element_mask, gradient, jnp.float32(0.0)), axis=(1, 2)))
        moved_diag = diag_values - step_length * along
        diag_values = 0.5 * (moved_diag + jnp.sqrt(moved_diag * moved_diag + 4.0 * step_length))
    return (stored, diag_values.reshape(-1), jnp.stack(objectives))
```

```python
import functools

import jax
import jax.numpy as jnp
from jax import lax
from jax.experimental import pallas as pl
from jax.experimental.pallas import tpu as pltpu
from jax.sharding import PartitionSpec as P

STEPS = 2


step_length = 0.5
penalty = 0.5
MESH = pl.DeviceIdType.MESH


def shrink(moved, level):
    return moved - jnp.clip(moved, -level, level)


def flip(index, offset, count):
    out, bit = 0, 1
    while bit < count:
        out = out + ((index // bit + offset // bit) % 2) * bit
        bit *= 2
    return out


def pack_kernel(samp, var, near_idx, far_idx, own_slot, x_ref, blk_hbm, dia_ref,
                near_ref, far_ref, own_ref, odia_ref, sem):
    width = dia_ref.shape[1]
    me = lax.axis_index("samp")
    copies = []
    for u in range(var):
        col = near_idx[u * samp + me]
        slot = own_slot[u * samp + me]
        for part in range(2):
            which = slot if part == 0 else 1 - slot
            copy = pltpu.make_async_copy(blk_hbm.at[col, which], own_ref.at[u, part], sem.at[u, part])
            copy.start()
            copies.append(copy)
        odia_ref[pl.ds(u, 1), :] = dia_ref[pl.ds(col, 1), :]
    for u in range(var):
        for k in range(samp):
            at = u * samp + k
            near = pl.multiple_of(near_idx[at] * width, width)
            near_ref[k, u] = x_ref[:, pl.ds(near, width)]
            far = pl.multiple_of(far_idx[at] * width, width)
            far_ref[u, k] = x_ref[:, pl.ds(far, width)]
    for copy in copies:
        copy.wait()


def main_kernel(samp, var, near_ref, far_ref, blk_ref, dia_ref, fin_ref, tails_ref, obj_ref,
                nearbuf, farz, farbuf, oz, acc,
                near_s, near_r, z_s, z_r, fwd_s, fwd_r, out_s, out_r,
                nloc, floc, zloc, tail_s, tail_r, oz_s, oz_r):
    s = lax.axis_index("samp")
    v = lax.axis_index("var")
    rows, width = near_ref.shape[2], near_ref.shape[3]
    total_rows = rows * samp

    barrier = pltpu.get_barrier_semaphore()
    for d in range(1, samp):
        pl.semaphore_signal(barrier, inc=1, device_id={"samp": flip(s, d, samp)}, device_id_type=MESH)
    for i in range(1, var):
        pl.semaphore_signal(barrier, inc=1, device_id={"var": flip(v, i, var)}, device_id_type=MESH)
    pl.semaphore_wait(barrier, samp + var - 2)

    def z_copy(i):
        u = flip(v, i, var)
        return pltpu.make_async_remote_copy(
            src_ref=far_ref.at[u], dst_ref=farz.at[v], send_sem=z_s.at[i], recv_sem=z_r.at[i],
            device_id={"var": u}, device_id_type=MESH)

    def near_copy(d, i):
        u, k = flip(v, i, var), flip(s, d, samp)
        return pltpu.make_async_remote_copy(
            src_ref=near_ref.at[k, u], dst_ref=nearbuf.at[s, u],
            send_sem=near_s.at[d, i], recv_sem=near_r.at[d, i],
            device_id={"samp": k}, device_id_type=MESH)

    def fwd_copy(d, i):
        u, k = flip(v, i, var), flip(s, d, samp)
        return pltpu.make_async_remote_copy(
            src_ref=farz.at[u, k], dst_ref=farbuf.at[u, s],
            send_sem=fwd_s.at[d, i], recv_sem=fwd_r.at[d, i],
            device_id={"samp": k}, device_id_type=MESH)

    def out_copy(d, i):
        u, k = flip(v, i, var), flip(s, d, samp)
        return pltpu.make_async_remote_copy(
            src_ref=fin_ref.at[s, u], dst_ref=fin_ref.at[s, u],
            send_sem=out_s.at[d, i], recv_sem=out_r.at[d, i],
            device_id={"samp": k}, device_id_type=MESH)

    def near_local(i):
        u = flip(v, i, var)
        return pltpu.make_async_copy(near_ref.at[s, u], nearbuf.at[s, u], nloc.at[i])

    def far_local(i):
        u = flip(v, i, var)
        return pltpu.make_async_copy(farz.at[u, s], farbuf.at[u, s], floc.at[i])

    def z_local():
        return pltpu.make_async_copy(far_ref.at[v], farz.at[v], zloc)

    def forward(i):
        for d in range(1, samp):
            fwd_copy(d, i).start()
        far_local(i).start()

    def start_near(i):
        for d in range(1, samp):
            near_copy(d, i).start()
        near_local(i).start()

    eye = lax.broadcasted_iota(jnp.int32, (width, width), 0) == lax.broadcasted_iota(
        jnp.int32, (width, width), 1)

    def column(i):
        u = flip(v, i, var)
        for d in range(1, samp):
            near_copy(d, i).wait_recv()
            fwd_copy(d, i).wait_recv()
        near_local(i).wait()
        far_local(i).wait()
        a = jnp.concatenate([nearbuf[p, u] for p in range(samp)], axis=0)
        b = jnp.concatenate([farbuf[u, p] for p in range(samp)], axis=0)
        wd = jnp.where(eye, 0.0, blk_ref[u, 0])
        wo = blk_ref[u, 1]
        dv = dia_ref[pl.ds(u, 1), :]
        over_first = (((0,), (0,)), ((), ()))
        for step in range(STEPS):
            rd = jnp.where(eye, dv, wd).astype(jnp.bfloat16)
            ro = wo.astype(jnp.bfloat16)
            product = jnp.dot(a, rd, preferred_element_type=jnp.float32)
            product = product + jnp.dot(b, ro, preferred_element_type=jnp.float32)
            terms = (jnp.sum(product * product, axis=0, keepdims=True) / (2.0 * total_rows)
                     - jnp.log(dv)
                     + penalty * jnp.sum(jnp.abs(wd) + jnp.abs(wo), axis=0, keepdims=True))
            acc[step:step + 1, :] += terms
            low = product.astype(jnp.bfloat16)
            gd = lax.dot_general(a, low, over_first, preferred_element_type=jnp.float32) / total_rows
            go = lax.dot_general(b, low, over_first, preferred_element_type=jnp.float32) / total_rows
            wo = shrink(wo - step_length * go, step_length * penalty)
            wd = jnp.where(eye, 0.0, shrink(wd - step_length * gd, step_length * penalty))
            along = jnp.sum(jnp.where(eye, gd, 0.0), axis=0, keepdims=True)
            moved = dv - step_length * along
            dv = 0.5 * (moved + jnp.sqrt(moved * moved + 4.0 * step_length))
        fin_ref[s, u, 0] = wd.astype(jnp.bfloat16)
        fin_ref[s, u, 1] = wo.astype(jnp.bfloat16)
        tails_ref[s, pl.ds(u, 1), :] = dv
        for d in range(1, samp):
            out_copy(d, i).start()

    acc[...] = jnp.zeros_like(acc)
    z_local().start()
    lax.fori_loop(1, var, lambda i, c: (z_copy(i).start(), c)[1], 0)
    start_near(0)
    z_local().wait()
    forward(0)
    lax.fori_loop(1, var, lambda i, c: (start_near(i), c)[1], 0)

    def turn(i, carry):
        @pl.when(i < var)
        def _():
            z_copy(i).wait_recv()
            forward(i)

        column(i - 1)
        return carry

    lax.fori_loop(1, var + 1, turn, 0)

    tails_ref[s, var:, :] = acc[...]

    def tail_copy(d):
        return pltpu.make_async_remote_copy(
            src_ref=tails_ref.at[s], dst_ref=tails_ref.at[s],
            send_sem=tail_s.at[d], recv_sem=tail_r.at[d],
            device_id={"samp": flip(s, d, samp)}, device_id_type=MESH)

    def oz_copy(i):
        return pltpu.make_async_remote_copy(
            src_ref=oz.at[v], dst_ref=oz.at[v], send_sem=oz_s.at[i], recv_sem=oz_r.at[i],
            device_id={"var": flip(v, i, var)}, device_id_type=MESH)

    for d in range(1, samp):
        tail_copy(d).start()
    for d in range(1, samp):
        tail_copy(d).wait_recv()
    group = tails_ref[0, var:, :]
    for k in range(1, samp):
        group = group + tails_ref[k, var:, :]
    oz[v] = group
    for i in range(1, var):
        oz_copy(i).start()
    for i in range(1, var):
        oz_copy(i).wait_recv()
    whole = oz[0]
    for u in range(1, var):
        whole = whole + oz[u]
    obj_ref[...] = whole

    def finish(i, carry):
        for d in range(1, samp):
            near_copy(d, i).wait_send()
            fwd_copy(d, i).wait_send()
            out_copy(d, i).wait()
        return carry

    lax.fori_loop(0, var, finish, 0)
    for d in range(1, samp):
        tail_copy(d).wait_send()
    for i in range(1, var):
        z_copy(i).wait_send()
        oz_copy(i).wait_send()


def unpack_kernel(group, owner, rank, slot, fin_ref, tails_ref, out_ref, dia_ref):
    first = pl.program_id(0) * group
    for j in range(group):
        col = first + j
        k, u, at = rank[col], owner[col], slot[col]
        out_ref[j, 0] = fin_ref[k, u, at].astype(jnp.float32)
        out_ref[j, 1] = fin_ref[k, u, 1 - at].astype(jnp.float32)
        dia_ref[pl.ds(col, 1), :] = tails_ref[k, pl.ds(u, 1), :]


def column_body(observed, blocks, diagonal, pattern):
    cols, width = blocks.shape[0], blocks.shape[2]
    rows = observed.shape[0]
    var, samp = lax.axis_size("var"), lax.axis_size("samp")
    v = lax.axis_index("var")
    ids = jnp.arange(cols, dtype=jnp.int32)
    on_diag = pattern == (v * cols + ids)[:, None]
    off_row = jnp.sum(jnp.where(on_diag, 0, pattern), axis=1)
    diag_slot = jnp.where(on_diag[:, 1], 1, 0).astype(jnp.int32)
    owner = off_row // cols
    resident = off_row % cols
    earlier = (owner[None, :] == owner[:, None]) & (ids[None, :] < ids[:, None])
    rank = jnp.sum(earlier, axis=1).astype(jnp.int32)
    slot_index = owner * samp + rank
    match = slot_index[:, None] == ids[None, :]
    wanted = jnp.sum(jnp.where(match, resident[:, None], 0), axis=0)
    near_idx = jnp.sum(jnp.where(match, ids[:, None], 0), axis=0)
    own_slot = jnp.sum(jnp.where(match, diag_slot[:, None], 0), axis=0)
    asked = lax.all_to_all(wanted, "var", split_axis=0, concat_axis=0, tiled=True)

    vmem = pl.BlockSpec(memory_space=pltpu.VMEM)
    smem = pl.BlockSpec(memory_space=pltpu.SMEM)
    hbm = pl.BlockSpec(memory_space=pl.ANY)
    near, far, own, own_dia = pl.pallas_call(
        functools.partial(pack_kernel, samp, var),
        out_shape=(
            jax.ShapeDtypeStruct((samp, var, rows, width), observed.dtype),
            jax.ShapeDtypeStruct((var, samp, rows, width), observed.dtype),
            jax.ShapeDtypeStruct((var, 2, width, width), jnp.float32),
            jax.ShapeDtypeStruct((var, width), jnp.float32),
        ),
        in_specs=[smem, smem, smem, vmem, hbm, vmem],
        out_specs=(vmem,) * 4,
        scratch_shapes=[pltpu.SemaphoreType.DMA((var, 2))],
        name="pack",
    )(near_idx, asked, own_slot, observed, blocks, diagonal.reshape(cols, width))

    dma = pltpu.SemaphoreType.DMA
    fin, tails, whole = pl.pallas_call(
        functools.partial(main_kernel, samp, var),
        out_shape=(
            jax.ShapeDtypeStruct((samp, var, 2, width, width), jnp.bfloat16),
            jax.ShapeDtypeStruct((samp, var + 8, width), jnp.float32),
            jax.ShapeDtypeStruct((8, width), jnp.float32),
        ),
        in_specs=[vmem] * 4,
        out_specs=(vmem,) * 3,
        scratch_shapes=[
            pltpu.VMEM((samp, var, rows, width), observed.dtype),
            pltpu.VMEM((var, samp, rows, width), observed.dtype),
            pltpu.VMEM((var, samp, rows, width), observed.dtype),
            pltpu.VMEM((var, 8, width), jnp.float32),
            pltpu.VMEM((8, width), jnp.float32),
            dma((samp, var)), dma((samp, var)), dma((var,)), dma((var,)),
            dma((samp, var)), dma((samp, var)), dma((samp, var)), dma((samp, var)),
            dma((var,)), dma((var,)), dma, dma((samp,)), dma((samp,)), dma((var,)), dma((var,)),
        ],
        compiler_params=pltpu.CompilerParams(collective_id=0, has_side_effects=True),
        name="columns",
    )(near, far, own, own_dia)

    group = 4
    new_blocks, new_diagonal = pl.pallas_call(
        functools.partial(unpack_kernel, group),
        out_shape=(
            jax.ShapeDtypeStruct(blocks.shape, jnp.float32),
            jax.ShapeDtypeStruct((cols, width), jnp.float32),
        ),
        grid=(cols // group,),
        in_specs=[smem, smem, smem, vmem, vmem],
        out_specs=(
            pl.BlockSpec((group, 2, width, width), lambda g: (g, 0, 0, 0)),
            pl.BlockSpec((cols, width), lambda g: (0, 0)),
        ),
        name="unpack",
    )(owner, rank, diag_slot, fin, tails)
    objective = jnp.sum(whole[:STEPS], axis=1) / (cols * width * var)
    return new_blocks, new_diagonal.reshape(-1), objective


def advance(diag_block, off_block, diag_values, grad_diag, grad_off, diag_mask, total_rows):
    grad_diag = grad_diag / total_rows
    grad_off = grad_off / total_rows
    new_off = shrink(off_block - step_length * grad_off, step_length * penalty)
    new_diag_block = jnp.where(
        diag_mask, 0.0, shrink(diag_block - step_length * grad_diag, step_length * penalty)
    )
    along = jnp.sum(jnp.where(diag_mask, grad_diag, 0.0), axis=1)
    moved = diag_values - step_length * along
    new_values = 0.5 * (moved + jnp.sqrt(moved * moved + 4.0 * step_length))
    return (new_diag_block, new_off, new_values)


def body(observed, blocks, diagonal, pattern):
    col_count = blocks.shape[0]
    block_width = blocks.shape[2]
    sample_rows = observed.shape[0]
    var_count = lax.axis_size("var")
    samp_count = lax.axis_size("samp")
    capacity = max(2, -(-col_count // var_count))
    total_rows = sample_rows * samp_count
    matrix_order = col_count * block_width * var_count
    var_index = lax.axis_index("var")
    column_ids = jnp.arange(col_count, dtype=jnp.int32)
    columns = var_index * col_count + column_ids
    on_diag = pattern == columns[:, None]
    off_row = jnp.sum(jnp.where(on_diag, 0, pattern), axis=1)
    owner_index = off_row // col_count
    resident_block = off_row % col_count
    earlier = (owner_index[None, :] == owner_index[:, None]) & (
        column_ids[None, :] < column_ids[:, None]
    )
    position_rank = jnp.sum(earlier, axis=1)
    slot_index = owner_index * capacity + position_rank
    all_slots = jnp.arange(var_count * capacity, dtype=jnp.int32)
    slot_match = slot_index[:, None] == all_slots[None, :]
    wanted = jnp.sum(jnp.where(slot_match, resident_block[:, None], 0), axis=0)
    asked_blocks = lax.all_to_all(wanted, "var", split_axis=0, concat_axis=0, tiled=True)
    nearby_panels = observed.reshape(sample_rows, col_count, block_width)
    outgoing = jnp.take(nearby_panels, asked_blocks, axis=1)
    arrived = lax.all_to_all(outgoing, "var", split_axis=1, concat_axis=1, tiled=True)
    distant_panels = jnp.take(arrived, slot_index, axis=1)
    diag_mask = jnp.eye(block_width, dtype=bool)
    flags = on_diag[:, :, None, None]
    diag_block = jnp.sum(jnp.where(flags, blocks, 0.0), axis=1)
    diag_block = jnp.where(diag_mask, 0.0, diag_block)
    off_block = jnp.sum(jnp.where(flags, 0.0, blocks), axis=1)
    diag_values = diagonal.reshape(col_count, block_width)
    samp_first = (lax.axis_index("samp") == 0).astype(jnp.float32)
    objective_parts = []
    for iteration in range(STEPS):
        full_diag = jnp.where(diag_mask, diag_values[:, None, :], diag_block)
        product = jnp.einsum(
            "qlh,lhy->qly",
            nearby_panels,
            full_diag.astype(jnp.bfloat16),
            preferred_element_type=jnp.float32,
        )
        product = product + jnp.einsum(
            "qlh,lhy->qly",
            distant_panels,
            off_block.astype(jnp.bfloat16),
            preferred_element_type=jnp.float32,
        )
        squares = jnp.sum(product * product)
        local_terms = -jnp.sum(jnp.log(diag_values)) + penalty * (
            jnp.sum(jnp.abs(diag_block)) + jnp.sum(jnp.abs(off_block))
        )
        part_value = (squares / (2.0 * total_rows) + samp_first * local_terms) / matrix_order
        objective_parts.append(part_value)
        lower_precision_product = product.astype(jnp.bfloat16)
        grad_diag = jnp.einsum(
            "rei,reo->eio",
            nearby_panels,
            lower_precision_product,
            preferred_element_type=jnp.float32,
        )
        grad_off = jnp.einsum(
            "rei,reo->eio",
            distant_panels,
            lower_precision_product,
            preferred_element_type=jnp.float32,
        )
        grad_diag, grad_off = lax.psum((grad_diag, grad_off), "samp")
        diag_block, off_block, diag_values = advance(
            diag_block, off_block, diag_values, grad_diag, grad_off, diag_mask, total_rows
        )
    objective = lax.psum(jnp.stack(objective_parts), ("samp", "var"))
    new_blocks = jnp.where(flags, diag_block[:, None], off_block[:, None])
    return (new_blocks, diag_values.reshape(-1), objective)


def power_of_two(count):
    return count & (count - 1) == 0


def whole_body(observed, blocks, diagonal, pattern):
    cols = blocks.shape[0]
    var, samp = lax.axis_size("var"), lax.axis_size("samp")
    exact = samp * var == cols and cols % 4 == 0 and var % 8 == 0 and blocks.shape[2] == 128
    if exact and power_of_two(samp) and power_of_two(var):
        return column_body(observed, blocks, diagonal, pattern)
    return body(observed, blocks, diagonal, pattern)


def solution(mesh):
    placed = (P("samp", "var"), P("var", None, None, None), P("var"), P("var", None))
    return jax.shard_map(
        whole_body,
        mesh=mesh,
        in_specs=placed,
        out_specs=(P("var", None, None, None), P("var"), P()),
        check_vma=False,
    )
```

```python
import functools

import jax
import jax.numpy as jnp
from jax import lax
from jax.experimental import pallas as pl
from jax.experimental.pallas import tpu as pltpu
from jax.sharding import PartitionSpec as P

STEPS = 2


step_length = 0.5
penalty = 0.5
MESH = pl.DeviceIdType.MESH


def shrink(moved, level):
    return moved - jnp.clip(moved, -level, level)


def flip(index, offset, count):
    out, bit = 0, 1
    while bit < count:
        out = out + ((index // bit + offset // bit) % 2) * bit
        bit *= 2
    return out


def ask_kernel(var, want_ref, asked_ref, got, send, recv):
    v = lax.axis_index("var")
    barrier = pltpu.get_barrier_semaphore()
    for i in range(1, var):
        pl.semaphore_signal(barrier, inc=1, device_id={"var": flip(v, i, var)}, device_id_type=MESH)
    pl.semaphore_wait(barrier, var - 1)

    def copy(i):
        u = flip(v, i, var)
        return pltpu.make_async_remote_copy(
            src_ref=want_ref.at[u], dst_ref=got.at[v], send_sem=send.at[i], recv_sem=recv.at[i],
            device_id={"var": u}, device_id_type=MESH)

    for i in range(1, var):
        copy(i).start()
    got[v] = want_ref[v]
    for i in range(1, var):
        copy(i).wait()
    asked_ref[...] = got[...]


def pack_kernel(samp, var, near_idx, far_idx, own_slot, x_ref, blk_hbm, dia_ref,
                near_ref, far_ref, own_ref, odia_ref, sem):
    width = dia_ref.shape[1]
    me = lax.axis_index("samp")
    copies = []
    for u in range(var):
        col = near_idx[u * samp + me]
        slot = own_slot[u * samp + me]
        for part in range(2):
            which = slot if part == 0 else 1 - slot
            copy = pltpu.make_async_copy(blk_hbm.at[col, which], own_ref.at[u, part], sem.at[u, part])
            copy.start()
            copies.append(copy)
        odia_ref[pl.ds(u, 1), :] = dia_ref[pl.ds(col, 1), :]
    for u in range(var):
        for k in range(samp):
            at = u * samp + k
            near = pl.multiple_of(near_idx[at] * width, width)
            near_ref[k, u] = x_ref[:, pl.ds(near, width)]
            far = pl.multiple_of(far_idx[u, 0, k] * width, width)
            far_ref[u, k] = x_ref[:, pl.ds(far, width)]
    for copy in copies:
        copy.wait()


def main_kernel(samp, var, near_ref, far_ref, blk_ref, dia_ref, fin_ref, tails_ref, obj_ref, farz, cc_out, cc_in, cc_own, oo_out, oo_in, oo_own, oz, acc,
                cc_s, cc_r, z_s, z_r, oo_s, oo_r, out_s, out_r,
                tail_s, tail_r, oz_s, oz_r):
    s = lax.axis_index("samp")
    v = lax.axis_index("var")
    rows, width = farz.shape[2], farz.shape[3]
    total_rows = rows * samp
    over_first = (((0,), (0,)), ((), ()))

    barrier = pltpu.get_barrier_semaphore()
    for i in range(1, var):
        pl.semaphore_signal(barrier, inc=1, device_id={"var": flip(v, i, var)}, device_id_type=MESH)
    for d in range(1, samp):
        pl.semaphore_signal(barrier, inc=1, device_id={"samp": flip(s, d, samp)}, device_id_type=MESH)
    pl.semaphore_wait(barrier, samp + var - 2)

    def remote(src, dst, send, recv, **where):
        return pltpu.make_async_remote_copy(
            src_ref=src, dst_ref=dst, send_sem=send, recv_sem=recv,
            device_id=where, device_id_type=MESH)

    def z_copy(i):
        u = flip(v, i, var)
        return remote(far_ref.at[u], farz.at[v], z_s.at[i], z_r.at[i], var=u)

    def cc_copy(d, i):
        u, k = flip(v, i, var), flip(s, d, samp)
        return remote(cc_out.at[u, k], cc_in.at[u, s], cc_s.at[d, i], cc_r.at[d, i], samp=k)

    def oo_copy(d, i):
        u, k = flip(v, i, var), flip(s, d, samp)
        return remote(oo_out.at[u, k], oo_in.at[u, s], oo_s.at[d, i], oo_r.at[d, i], samp=k)

    def out_copy(d, i):
        u, k = flip(v, i, var), flip(s, d, samp)
        return remote(fin_ref.at[s, u], fin_ref.at[s, u], out_s.at[d, i], out_r.at[d, i], samp=k)

    def gram(left, right):
        return lax.dot_general(left, right, over_first, preferred_element_type=jnp.float32)

    def start_cc(i):
        u = flip(v, i, var)
        for d in range(samp):
            k = flip(s, d, samp)
            c = near_ref[k, u]
            part = gram(c, c)
            if d == 0:
                cc_own[u] = part
            else:
                cc_out[u, k] = part.astype(jnp.bfloat16)
                cc_copy(d, i).start()

    def start_oo(i, far_panel):
        u = flip(v, i, var)
        for d in range(samp):
            k = flip(s, d, samp)
            o = far_panel(u, k)
            part = gram(o, jnp.concatenate([near_ref[k, u], o], axis=1))
            if d == 0:
                oo_own[u] = part
            else:
                oo_out[u, k] = part.astype(jnp.bfloat16)
                oo_copy(d, i).start()

    eye = lax.broadcasted_iota(jnp.int32, (width, width), 0) == lax.broadcasted_iota(
        jnp.int32, (width, width), 1)

    def column(i):
        u = flip(v, i, var)
        for d in range(1, samp):
            cc_copy(d, i).wait_recv()
            oo_copy(d, i).wait_recv()
        cc, oo = cc_own[u], oo_own[u]
        for d in range(1, samp):
            p = flip(s, d, samp)
            cc = cc + cc_in[u, p].astype(jnp.float32)
            oo = oo + oo_in[u, p].astype(jnp.float32)
        both = jnp.concatenate(
            [jnp.concatenate([cc, oo[:, :width].T], axis=1), oo], axis=0)
        high = both.astype(jnp.bfloat16)
        low = (both - high.astype(jnp.float32)).astype(jnp.bfloat16)
        gram_parts = jnp.concatenate([high, low], axis=1)
        wd = jnp.where(eye, 0.0, blk_ref[u, 0])
        wo = blk_ref[u, 1]
        dv = dia_ref[pl.ds(u, 1), :]
        for step in range(STEPS):
            rounded = jnp.concatenate(
                [jnp.where(eye, dv, wd).astype(jnp.bfloat16), wo.astype(jnp.bfloat16)], axis=0)
            grad = jnp.dot(gram_parts, jnp.concatenate([rounded, rounded], axis=0),
                           preferred_element_type=jnp.float32)
            squares = jnp.sum(grad * rounded.astype(jnp.float32), axis=0, keepdims=True)
            terms = (squares / (2.0 * total_rows) - jnp.log(dv)
                     + penalty * jnp.sum(jnp.abs(wd) + jnp.abs(wo), axis=0, keepdims=True))
            acc[step:step + 1, :] += terms
            grad = grad / total_rows
            gd, go = grad[:width], grad[width:]
            wo = shrink(wo - step_length * go, step_length * penalty)
            wd = jnp.where(eye, 0.0, shrink(wd - step_length * gd, step_length * penalty))
            along = jnp.sum(jnp.where(eye, gd, 0.0), axis=0, keepdims=True)
            moved = dv - step_length * along
            dv = 0.5 * (moved + jnp.sqrt(moved * moved + 4.0 * step_length))
        fin_ref[s, u, 0] = wd.astype(jnp.bfloat16)
        fin_ref[s, u, 1] = wo.astype(jnp.bfloat16)
        tails_ref[s, pl.ds(u, 1), :] = dv
        for d in range(1, samp):
            out_copy(d, i).start()

    acc[...] = jnp.zeros_like(acc)
    for i in range(1, var):
        z_copy(i).start()
    start_cc(0)
    start_oo(0, lambda u, k: far_ref[v, k])
    lax.fori_loop(1, var, lambda i, c: (start_cc(i), c)[1], 0)

    def turn(i, carry):
        @pl.when(i < var)
        def _():
            z_copy(i).wait_recv()
            start_oo(i, lambda u, k: farz[u, k])

        column(i - 1)
        return carry

    lax.fori_loop(1, var + 1, turn, 0)

    tails_ref[s, var:, :] = acc[...]

    def tail_copy(d):
        return remote(tails_ref.at[s], tails_ref.at[s], tail_s.at[d], tail_r.at[d],
                      samp=flip(s, d, samp))

    def oz_copy(i):
        return remote(oz.at[v], oz.at[v], oz_s.at[i], oz_r.at[i], var=flip(v, i, var))

    for d in range(1, samp):
        tail_copy(d).start()
    for d in range(1, samp):
        tail_copy(d).wait_recv()
    group = tails_ref[0, var:, :]
    for k in range(1, samp):
        group = group + tails_ref[k, var:, :]
    oz[v] = group
    for i in range(1, var):
        oz_copy(i).start()
    for i in range(1, var):
        oz_copy(i).wait_recv()
    whole = oz[0]
    for u in range(1, var):
        whole = whole + oz[u]
    obj_ref[...] = whole

    def finish(i, carry):
        for d in range(1, samp):
            cc_copy(d, i).wait_send()
            oo_copy(d, i).wait_send()
            out_copy(d, i).wait()
        return carry

    lax.fori_loop(0, var, finish, 0)
    for d in range(1, samp):
        tail_copy(d).wait_send()
    for i in range(1, var):
        z_copy(i).wait_send()
        oz_copy(i).wait_send()


def unpack_kernel(group, owner, rank, slot, fin_ref, tails_ref, out_ref, dia_ref):
    first = pl.program_id(0) * group
    for j in range(group):
        col = first + j
        k, u, at = rank[col], owner[col], slot[col]
        out_ref[j, 0] = fin_ref[k, u, at].astype(jnp.float32)
        out_ref[j, 1] = fin_ref[k, u, 1 - at].astype(jnp.float32)
        dia_ref[pl.ds(col, 1), :] = tails_ref[k, pl.ds(u, 1), :]


def column_body(observed, blocks, diagonal, pattern):
    cols, width = blocks.shape[0], blocks.shape[2]
    rows = observed.shape[0]
    var, samp = lax.axis_size("var"), lax.axis_size("samp")
    v = lax.axis_index("var")
    ids = jnp.arange(cols, dtype=jnp.int32)
    on_diag = pattern == (v * cols + ids)[:, None]
    off_row = jnp.sum(jnp.where(on_diag, 0, pattern), axis=1)
    diag_slot = jnp.where(on_diag[:, 1], 1, 0).astype(jnp.int32)
    owner = off_row // cols
    resident = off_row % cols
    earlier = (owner[None, :] == owner[:, None]) & (ids[None, :] < ids[:, None])
    rank = jnp.sum(earlier, axis=1).astype(jnp.int32)
    slot_index = owner * samp + rank
    match = slot_index[:, None] == ids[None, :]
    wanted = jnp.sum(jnp.where(match, resident[:, None], 0), axis=0)
    near_idx = jnp.sum(jnp.where(match, ids[:, None], 0), axis=0)
    own_slot = jnp.sum(jnp.where(match, diag_slot[:, None], 0), axis=0)
    want = jnp.pad(wanted.reshape(var, 1, samp), ((0, 0), (0, 0), (0, width - samp)))

    vmem = pl.BlockSpec(memory_space=pltpu.VMEM)
    smem = pl.BlockSpec(memory_space=pltpu.SMEM)
    hbm = pl.BlockSpec(memory_space=pl.ANY)
    dma = pltpu.SemaphoreType.DMA
    bf16, f32 = jnp.bfloat16, jnp.float32
    asked = pl.pallas_call(
        functools.partial(ask_kernel, var),
        out_shape=jax.ShapeDtypeStruct((var, 1, width), jnp.int32),
        in_specs=[vmem],
        out_specs=vmem,
        scratch_shapes=[pltpu.VMEM((var, 1, width), jnp.int32), dma((var,)), dma((var,))],
        compiler_params=pltpu.CompilerParams(collective_id=1, has_side_effects=True),
        name="ask",
    )(want)
    near, far, own, own_dia = pl.pallas_call(
        functools.partial(pack_kernel, samp, var),
        out_shape=(
            jax.ShapeDtypeStruct((samp, var, rows, width), observed.dtype),
            jax.ShapeDtypeStruct((var, samp, rows, width), observed.dtype),
            jax.ShapeDtypeStruct((var, 2, width, width), f32),
            jax.ShapeDtypeStruct((var, width), f32),
        ),
        in_specs=[smem, smem, smem, vmem, hbm, vmem],
        out_specs=(vmem,) * 4,
        scratch_shapes=[dma((var, 2))],
        name="pack",
    )(near_idx, asked, own_slot, observed, blocks, diagonal.reshape(cols, width))
    fin, tails, whole = pl.pallas_call(
        functools.partial(main_kernel, samp, var),
        out_shape=(
            jax.ShapeDtypeStruct((samp, var, 2, width, width), bf16),
            jax.ShapeDtypeStruct((samp, var + 8, width), f32),
            jax.ShapeDtypeStruct((8, width), f32),
        ),
        in_specs=[vmem] * 4,
        out_specs=(vmem,) * 3,
        scratch_shapes=[
            pltpu.VMEM((var, samp, rows, width), observed.dtype),
            pltpu.VMEM((var, samp, width, width), bf16),
            pltpu.VMEM((var, samp, width, width), bf16),
            pltpu.VMEM((var, width, width), f32),
            pltpu.VMEM((var, samp, width, 2 * width), bf16),
            pltpu.VMEM((var, samp, width, 2 * width), bf16),
            pltpu.VMEM((var, width, 2 * width), f32),
            pltpu.VMEM((var, 8, width), f32),
            pltpu.VMEM((8, width), f32),
            dma((samp, var)), dma((samp, var)), dma((var,)), dma((var,)),
            dma((samp, var)), dma((samp, var)), dma((samp, var)), dma((samp, var)),
            dma((samp,)), dma((samp,)), dma((var,)), dma((var,)),
        ],
        compiler_params=pltpu.CompilerParams(collective_id=0, has_side_effects=True),
        name="columns",
    )(near, far, own, own_dia)

    group = 4
    new_blocks, new_diagonal = pl.pallas_call(
        functools.partial(unpack_kernel, group),
        out_shape=(
            jax.ShapeDtypeStruct(blocks.shape, jnp.float32),
            jax.ShapeDtypeStruct((cols, width), jnp.float32),
        ),
        grid=(cols // group,),
        in_specs=[smem, smem, smem, vmem, vmem],
        out_specs=(
            pl.BlockSpec((group, 2, width, width), lambda g: (g, 0, 0, 0)),
            pl.BlockSpec((cols, width), lambda g: (0, 0)),
        ),
        name="unpack",
    )(owner, rank, diag_slot, fin, tails)
    objective = jnp.sum(whole[:STEPS], axis=1) / (cols * width * var)
    return new_blocks, new_diagonal.reshape(-1), objective


def advance(diag_block, off_block, diag_values, grad_diag, grad_off, diag_mask, total_rows):
    grad_diag = grad_diag / total_rows
    grad_off = grad_off / total_rows
    new_off = shrink(off_block - step_length * grad_off, step_length * penalty)
    new_diag_block = jnp.where(
        diag_mask, 0.0, shrink(diag_block - step_length * grad_diag, step_length * penalty)
    )
    along = jnp.sum(jnp.where(diag_mask, grad_diag, 0.0), axis=1)
    moved = diag_values - step_length * along
    new_values = 0.5 * (moved + jnp.sqrt(moved * moved + 4.0 * step_length))
    return (new_diag_block, new_off, new_values)


def body(observed, blocks, diagonal, pattern):
    col_count = blocks.shape[0]
    block_width = blocks.shape[2]
    sample_rows = observed.shape[0]
    var_count = lax.axis_size("var")
    samp_count = lax.axis_size("samp")
    capacity = max(2, -(-col_count // var_count))
    total_rows = sample_rows * samp_count
    matrix_order = col_count * block_width * var_count
    var_index = lax.axis_index("var")
    column_ids = jnp.arange(col_count, dtype=jnp.int32)
    columns = var_index * col_count + column_ids
    on_diag = pattern == columns[:, None]
    off_row = jnp.sum(jnp.where(on_diag, 0, pattern), axis=1)
    owner_index = off_row // col_count
    resident_block = off_row % col_count
    earlier = (owner_index[None, :] == owner_index[:, None]) & (
        column_ids[None, :] < column_ids[:, None]
    )
    position_rank = jnp.sum(earlier, axis=1)
    slot_index = owner_index * capacity + position_rank
    all_slots = jnp.arange(var_count * capacity, dtype=jnp.int32)
    slot_match = slot_index[:, None] == all_slots[None, :]
    wanted = jnp.sum(jnp.where(slot_match, resident_block[:, None], 0), axis=0)
    asked_blocks = lax.all_to_all(wanted, "var", split_axis=0, concat_axis=0, tiled=True)
    nearby_panels = observed.reshape(sample_rows, col_count, block_width)
    outgoing = jnp.take(nearby_panels, asked_blocks, axis=1)
    arrived = lax.all_to_all(outgoing, "var", split_axis=1, concat_axis=1, tiled=True)
    distant_panels = jnp.take(arrived, slot_index, axis=1)
    diag_mask = jnp.eye(block_width, dtype=bool)
    flags = on_diag[:, :, None, None]
    diag_block = jnp.sum(jnp.where(flags, blocks, 0.0), axis=1)
    diag_block = jnp.where(diag_mask, 0.0, diag_block)
    off_block = jnp.sum(jnp.where(flags, 0.0, blocks), axis=1)
    diag_values = diagonal.reshape(col_count, block_width)
    samp_first = (lax.axis_index("samp") == 0).astype(jnp.float32)
    objective_parts = []
    for iteration in range(STEPS):
        full_diag = jnp.where(diag_mask, diag_values[:, None, :], diag_block)
        product = jnp.einsum(
            "qlh,lhy->qly",
            nearby_panels,
            full_diag.astype(jnp.bfloat16),
            preferred_element_type=jnp.float32,
        )
        product = product + jnp.einsum(
            "qlh,lhy->qly",
            distant_panels,
            off_block.astype(jnp.bfloat16),
            preferred_element_type=jnp.float32,
        )
        squares = jnp.sum(product * product)
        local_terms = -jnp.sum(jnp.log(diag_values)) + penalty * (
            jnp.sum(jnp.abs(diag_block)) + jnp.sum(jnp.abs(off_block))
        )
        part_value = (squares / (2.0 * total_rows) + samp_first * local_terms) / matrix_order
        objective_parts.append(part_value)
        lower_precision_product = product.astype(jnp.bfloat16)
        grad_diag = jnp.einsum(
            "rei,reo->eio",
            nearby_panels,
            lower_precision_product,
            preferred_element_type=jnp.float32,
        )
        grad_off = jnp.einsum(
            "rei,reo->eio",
            distant_panels,
            lower_precision_product,
            preferred_element_type=jnp.float32,
        )
        grad_diag, grad_off = lax.psum((grad_diag, grad_off), "samp")
        diag_block, off_block, diag_values = advance(
            diag_block, off_block, diag_values, grad_diag, grad_off, diag_mask, total_rows
        )
    objective = lax.psum(jnp.stack(objective_parts), ("samp", "var"))
    new_blocks = jnp.where(flags, diag_block[:, None], off_block[:, None])
    return (new_blocks, diag_values.reshape(-1), objective)


def power_of_two(count):
    return count & (count - 1) == 0


def whole_body(observed, blocks, diagonal, pattern):
    cols = blocks.shape[0]
    var, samp = lax.axis_size("var"), lax.axis_size("samp")
    exact = samp * var == cols and cols % 4 == 0 and var % 8 == 0 and blocks.shape[2] == 128
    if exact and power_of_two(samp) and power_of_two(var):
        return column_body(observed, blocks, diagonal, pattern)
    return body(observed, blocks, diagonal, pattern)


def solution(mesh):
    placed = (P("samp", "var"), P("var", None, None, None), P("var"), P("var", None))
    return jax.shard_map(
        whole_body,
        mesh=mesh,
        in_specs=placed,
        out_specs=(P("var", None, None, None), P("var"), P()),
        check_vma=False,
    )
```

```python
import functools

import jax
import jax.numpy as jnp
from jax import lax
from jax.experimental import pallas as pl
from jax.experimental.pallas import tpu as pltpu
from jax.sharding import PartitionSpec as P

STEPS = 2


step_length = 0.5
penalty = 0.5
MESH = pl.DeviceIdType.MESH


def shrink(moved, level):
    return moved - jnp.clip(moved, -level, level)


def flip(index, offset, count):
    out, bit = 0, 1
    while bit < count:
        out = out + ((index // bit + offset // bit) % 2) * bit
        bit *= 2
    return out


def main_kernel(samp, var, near_idx, wanted, own_slot, want_ref, x_hbm, blk_hbm, dia_ref,
                fin_ref, tails_ref, obj_ref,
                x, blk, ask, ask_s, far, farz, cc_out, cc_in, cc_own, oo_out, oo_in, oo_own, oz, acc,
                load, ask_ss, ask_rs, ask_l, cc_s, cc_r, z_s, z_r, oo_s, oo_r, out_s, out_r,
                tail_s, tail_r, oz_s, oz_r):
    s = lax.axis_index("samp")
    v = lax.axis_index("var")
    rows, width = x.shape[1], x.shape[2]
    total_rows = rows * samp
    over_first = (((0,), (0,)), ((), ()))

    cols = x.shape[0]
    x_loads = [
        pltpu.make_async_copy(x_hbm.at[:, l * width:(l + 1) * width], x.at[l], load.at[l])
        for l in range(cols)
    ]
    for x_load in x_loads:
        x_load.start()
    blk_load = pltpu.make_async_copy(blk_hbm, blk, load.at[cols])
    blk_load.start()

    barrier = pltpu.get_barrier_semaphore()
    for i in range(1, var):
        pl.semaphore_signal(barrier, inc=1, device_id={"var": flip(v, i, var)}, device_id_type=MESH)
    for d in range(1, samp):
        pl.semaphore_signal(barrier, inc=1, device_id={"samp": flip(s, d, samp)}, device_id_type=MESH)
    pl.semaphore_wait(barrier, samp + var - 2)

    def remote(src, dst, send, recv, **where):
        return pltpu.make_async_remote_copy(
            src_ref=src, dst_ref=dst, send_sem=send, recv_sem=recv,
            device_id=where, device_id_type=MESH)

    def ask_copy(i):
        u = flip(v, i, var)
        return remote(want_ref.at[u], ask.at[v], ask_ss.at[i], ask_rs.at[i], var=u)

    def z_copy(i):
        u = flip(v, i, var)
        return remote(far.at[u], farz.at[v], z_s.at[i], z_r.at[i], var=u)

    def cc_copy(d, i):
        u, k = flip(v, i, var), flip(s, d, samp)
        return remote(cc_out.at[u, k], cc_in.at[u, s], cc_s.at[d, i], cc_r.at[d, i], samp=k)

    def oo_copy(d, i):
        u, k = flip(v, i, var), flip(s, d, samp)
        return remote(oo_out.at[u, k], oo_in.at[u, s], oo_s.at[d, i], oo_r.at[d, i], samp=k)

    def out_copy(d, i):
        u, k = flip(v, i, var), flip(s, d, samp)
        return remote(fin_ref.at[s, u], fin_ref.at[s, u], out_s.at[d, i], out_r.at[d, i], samp=k)

    def panel(index):
        return x[index]

    def near_panel(u, k):
        return panel(near_idx[u * samp + k])

    def gram(left, right):
        return lax.dot_general(left, right, over_first, preferred_element_type=jnp.float32)

    eye = lax.broadcasted_iota(jnp.int32, (width, width), 0) == lax.broadcasted_iota(
        jnp.int32, (width, width), 1)

    def residual(part):
        off = jnp.where(eye, part - part.astype(jnp.bfloat16).astype(jnp.float32), 0.0)
        row = jnp.sum(off, axis=0, keepdims=True)
        return jnp.broadcast_to(row, (16, width)).astype(jnp.bfloat16)

    def restored(block, rest):
        return block.astype(jnp.float32) + jnp.where(eye, rest.astype(jnp.float32)[:1], 0.0)

    def start_cc(i):
        u = flip(v, i, var)
        for d in range(samp):
            k = flip(s, d, samp)
            c = near_panel(u, k)
            part = gram(c, c)
            if d == 0:
                cc_own[u] = part
            else:
                cc_out[u, k, :width] = part.astype(jnp.bfloat16)
                cc_out[u, k, width:] = residual(part)
                cc_copy(d, i).start()

    def start_oo(i, far_panel):
        u = flip(v, i, var)
        for d in range(samp):
            k = flip(s, d, samp)
            o = far_panel(u, k)
            part = gram(o, jnp.concatenate([near_panel(u, k), o], axis=1))
            if d == 0:
                oo_own[u] = part
            else:
                oo_out[u, k, :width] = part.astype(jnp.bfloat16)
                rest = residual(part[:, width:])
                oo_out[u, k, width:] = jnp.concatenate([rest, rest], axis=1)
                oo_copy(d, i).start()

    def column(i):
        u = flip(v, i, var)
        for d in range(1, samp):
            cc_copy(d, i).wait_recv()
            oo_copy(d, i).wait_recv()
        cc, oc, oo = cc_own[u], oo_own[u, :, :width], oo_own[u, :, width:]
        for d in range(1, samp):
            p = flip(s, d, samp)
            cc = cc + restored(cc_in[u, p, :width], cc_in[u, p, width:])
            oc = oc + oo_in[u, p, :width, :width].astype(jnp.float32)
            oo = oo + restored(oo_in[u, p, :width, width:], oo_in[u, p, width:, width:])
        both = jnp.concatenate(
            [jnp.concatenate([cc, oc.T], axis=1), jnp.concatenate([oc, oo], axis=1)], axis=0)
        high = both.astype(jnp.bfloat16)
        low = (both - high.astype(jnp.float32)).astype(jnp.bfloat16)
        gram_parts = jnp.concatenate([high, low], axis=1)
        col = near_idx[u * samp + s]
        slot = own_slot[u * samp + s]
        wd = jnp.where(eye, 0.0, blk[col, slot])
        wo = blk[col, 1 - slot]
        dv = dia_ref[col]
        for step in range(STEPS):
            rounded = jnp.concatenate(
                [jnp.where(eye, dv, wd).astype(jnp.bfloat16), wo.astype(jnp.bfloat16)], axis=0)
            grad = jnp.dot(gram_parts, jnp.concatenate([rounded, rounded], axis=0),
                           preferred_element_type=jnp.float32)
            squares = jnp.sum(grad * rounded.astype(jnp.float32), axis=0, keepdims=True)
            terms = (squares / (2.0 * total_rows) - jnp.log(dv)
                     + penalty * jnp.sum(jnp.abs(wd) + jnp.abs(wo), axis=0, keepdims=True))
            acc[step:step + 1, :] += terms
            grad = grad / total_rows
            gd, go = grad[:width], grad[width:]
            wo = shrink(wo - step_length * go, step_length * penalty)
            wd = jnp.where(eye, 0.0, shrink(wd - step_length * gd, step_length * penalty))
            along = jnp.sum(jnp.where(eye, gd, 0.0), axis=0, keepdims=True)
            moved = dv - step_length * along
            dv = 0.5 * (moved + jnp.sqrt(moved * moved + 4.0 * step_length))
        fin_ref[s, u, 0] = wd.astype(jnp.bfloat16)
        fin_ref[s, u, 1] = wo.astype(jnp.bfloat16)
        tails_ref[s, pl.ds(u, 1), :] = dv
        for d in range(1, samp):
            out_copy(d, i).start()

    for i in range(1, var):
        ask_copy(i).start()
    acc[...] = jnp.zeros_like(acc)
    for x_load in x_loads:
        x_load.wait()
    start_cc(0)
    for i in range(1, var):
        ask_copy(i).wait_recv()
    ask[v] = want_ref[v]
    ask_load = pltpu.make_async_copy(ask, ask_s, ask_l)
    ask_load.start()
    ask_load.wait()

    def send_far(i, carry):
        u = flip(v, i, var)
        for k in range(samp):
            far[u, k] = panel(ask_s[u, 0, k])
        z_copy(i).start()
        return carry

    lax.fori_loop(1, var, send_far, 0)
    start_oo(0, lambda u, k: panel(wanted[u * samp + k]))
    lax.fori_loop(1, var, lambda i, c: (start_cc(i), c)[1], 0)
    blk_load.wait()

    def turn(i, carry):
        @pl.when(i < var)
        def _():
            z_copy(i).wait_recv()
            start_oo(i, lambda u, k: farz[u, k])

        column(i - 1)
        return carry

    lax.fori_loop(1, var + 1, turn, 0)

    tails_ref[s, var:, :] = acc[...]

    def tail_copy(d):
        return remote(tails_ref.at[s], tails_ref.at[s], tail_s.at[d], tail_r.at[d],
                      samp=flip(s, d, samp))

    def oz_copy(i):
        return remote(oz.at[v], oz.at[v], oz_s.at[i], oz_r.at[i], var=flip(v, i, var))

    for d in range(1, samp):
        tail_copy(d).start()
    for d in range(1, samp):
        tail_copy(d).wait_recv()
    group = tails_ref[0, var:, :]
    for k in range(1, samp):
        group = group + tails_ref[k, var:, :]
    oz[v] = group
    for i in range(1, var):
        oz_copy(i).start()
    for i in range(1, var):
        oz_copy(i).wait_recv()
    whole = oz[0]
    for u in range(1, var):
        whole = whole + oz[u]
    obj_ref[...] = whole

    def finish(i, carry):
        for d in range(1, samp):
            cc_copy(d, i).wait_send()
            oo_copy(d, i).wait_send()
            out_copy(d, i).wait()
        return carry

    lax.fori_loop(0, var, finish, 0)
    for d in range(1, samp):
        tail_copy(d).wait_send()
    for i in range(1, var):
        ask_copy(i).wait_send()
        z_copy(i).wait_send()
        oz_copy(i).wait_send()


def unpack_kernel(group, owner, rank, slot, fin_ref, tails_ref, out_ref, dia_ref):
    first = pl.program_id(0) * group
    for j in range(group):
        col = first + j
        k, u, at = rank[col], owner[col], slot[col]
        out_ref[j, 0] = fin_ref[k, u, at].astype(jnp.float32)
        out_ref[j, 1] = fin_ref[k, u, 1 - at].astype(jnp.float32)
        dia_ref[pl.ds(col, 1), :] = tails_ref[k, pl.ds(u, 1), :]


def column_body(observed, blocks, diagonal, pattern):
    cols, width = blocks.shape[0], blocks.shape[2]
    rows = observed.shape[0]
    var, samp = lax.axis_size("var"), lax.axis_size("samp")
    v = lax.axis_index("var")
    ids = jnp.arange(cols, dtype=jnp.int32)
    on_diag = pattern == (v * cols + ids)[:, None]
    off_row = jnp.sum(jnp.where(on_diag, 0, pattern), axis=1)
    diag_slot = jnp.where(on_diag[:, 1], 1, 0).astype(jnp.int32)
    owner = off_row // cols
    resident = off_row % cols
    earlier = (owner[None, :] == owner[:, None]) & (ids[None, :] < ids[:, None])
    rank = jnp.sum(earlier, axis=1).astype(jnp.int32)
    slot_index = owner * samp + rank
    match = slot_index[:, None] == ids[None, :]
    wanted = jnp.sum(jnp.where(match, resident[:, None], 0), axis=0)
    near_idx = jnp.sum(jnp.where(match, ids[:, None], 0), axis=0)
    own_slot = jnp.sum(jnp.where(match, diag_slot[:, None], 0), axis=0)
    want = jnp.pad(wanted.reshape(var, 1, samp), ((0, 0), (0, 0), (0, width - samp)))

    vmem = pl.BlockSpec(memory_space=pltpu.VMEM)
    smem = pl.BlockSpec(memory_space=pltpu.SMEM)
    hbm = pl.BlockSpec(memory_space=pl.ANY)
    dma = pltpu.SemaphoreType.DMA
    bf16, f32 = jnp.bfloat16, jnp.float32
    fin, tails, whole = pl.pallas_call(
        functools.partial(main_kernel, samp, var),
        out_shape=(
            jax.ShapeDtypeStruct((samp, var, 2, width, width), bf16),
            jax.ShapeDtypeStruct((samp, var + 8, width), f32),
            jax.ShapeDtypeStruct((8, width), f32),
        ),
        in_specs=[smem, smem, smem, vmem, hbm, hbm, vmem],
        out_specs=(vmem,) * 3,
        scratch_shapes=[
            pltpu.VMEM((cols, rows, width), observed.dtype),
            pltpu.VMEM(blocks.shape, f32),
            pltpu.VMEM((var, 1, width), jnp.int32),
            pltpu.SMEM((var, 1, width), jnp.int32),
            pltpu.VMEM((var, samp, rows, width), observed.dtype),
            pltpu.VMEM((var, samp, rows, width), observed.dtype),
            pltpu.VMEM((var, samp, width + 16, width), bf16),
            pltpu.VMEM((var, samp, width + 16, width), bf16),
            pltpu.VMEM((var, width, width), f32),
            pltpu.VMEM((var, samp, width + 16, 2 * width), bf16),
            pltpu.VMEM((var, samp, width + 16, 2 * width), bf16),
            pltpu.VMEM((var, width, 2 * width), f32),
            pltpu.VMEM((var, 8, width), f32),
            pltpu.VMEM((8, width), f32),
            dma((cols + 1,)), dma((var,)), dma((var,)), dma,
            dma((samp, var)), dma((samp, var)), dma((var,)), dma((var,)),
            dma((samp, var)), dma((samp, var)), dma((samp, var)), dma((samp, var)),
            dma((samp,)), dma((samp,)), dma((var,)), dma((var,)),
        ],
        compiler_params=pltpu.CompilerParams(collective_id=0, has_side_effects=True),
        name="columns",
    )(near_idx, wanted, own_slot, want, observed, blocks, diagonal.reshape(cols, 1, width))

    group = 4
    new_blocks, new_diagonal = pl.pallas_call(
        functools.partial(unpack_kernel, group),
        out_shape=(
            jax.ShapeDtypeStruct(blocks.shape, jnp.float32),
            jax.ShapeDtypeStruct((cols, width), jnp.float32),
        ),
        grid=(cols // group,),
        in_specs=[smem, smem, smem, vmem, vmem],
        out_specs=(
            pl.BlockSpec((group, 2, width, width), lambda g: (g, 0, 0, 0)),
            pl.BlockSpec((cols, width), lambda g: (0, 0)),
        ),
        name="unpack",
    )(owner, rank, diag_slot, fin, tails)
    objective = jnp.sum(whole[:STEPS], axis=1) / (cols * width * var)
    return new_blocks, new_diagonal.reshape(-1), objective


def advance(diag_block, off_block, diag_values, grad_diag, grad_off, diag_mask, total_rows):
    grad_diag = grad_diag / total_rows
    grad_off = grad_off / total_rows
    new_off = shrink(off_block - step_length * grad_off, step_length * penalty)
    new_diag_block = jnp.where(
        diag_mask, 0.0, shrink(diag_block - step_length * grad_diag, step_length * penalty)
    )
    along = jnp.sum(jnp.where(diag_mask, grad_diag, 0.0), axis=1)
    moved = diag_values - step_length * along
    new_values = 0.5 * (moved + jnp.sqrt(moved * moved + 4.0 * step_length))
    return (new_diag_block, new_off, new_values)


def body(observed, blocks, diagonal, pattern):
    col_count = blocks.shape[0]
    block_width = blocks.shape[2]
    sample_rows = observed.shape[0]
    var_count = lax.axis_size("var")
    samp_count = lax.axis_size("samp")
    capacity = max(2, -(-col_count // var_count))
    total_rows = sample_rows * samp_count
    matrix_order = col_count * block_width * var_count
    var_index = lax.axis_index("var")
    column_ids = jnp.arange(col_count, dtype=jnp.int32)
    columns = var_index * col_count + column_ids
    on_diag = pattern == columns[:, None]
    off_row = jnp.sum(jnp.where(on_diag, 0, pattern), axis=1)
    owner_index = off_row // col_count
    resident_block = off_row % col_count
    earlier = (owner_index[None, :] == owner_index[:, None]) & (
        column_ids[None, :] < column_ids[:, None]
    )
    position_rank = jnp.sum(earlier, axis=1)
    slot_index = owner_index * capacity + position_rank
    all_slots = jnp.arange(var_count * capacity, dtype=jnp.int32)
    slot_match = slot_index[:, None] == all_slots[None, :]
    wanted = jnp.sum(jnp.where(slot_match, resident_block[:, None], 0), axis=0)
    asked_blocks = lax.all_to_all(wanted, "var", split_axis=0, concat_axis=0, tiled=True)
    nearby_panels = observed.reshape(sample_rows, col_count, block_width)
    outgoing = jnp.take(nearby_panels, asked_blocks, axis=1)
    arrived = lax.all_to_all(outgoing, "var", split_axis=1, concat_axis=1, tiled=True)
    distant_panels = jnp.take(arrived, slot_index, axis=1)
    diag_mask = jnp.eye(block_width, dtype=bool)
    flags = on_diag[:, :, None, None]
    diag_block = jnp.sum(jnp.where(flags, blocks, 0.0), axis=1)
    diag_block = jnp.where(diag_mask, 0.0, diag_block)
    off_block = jnp.sum(jnp.where(flags, 0.0, blocks), axis=1)
    diag_values = diagonal.reshape(col_count, block_width)
    samp_first = (lax.axis_index("samp") == 0).astype(jnp.float32)
    objective_parts = []
    for iteration in range(STEPS):
        full_diag = jnp.where(diag_mask, diag_values[:, None, :], diag_block)
        product = jnp.einsum(
            "qlh,lhy->qly",
            nearby_panels,
            full_diag.astype(jnp.bfloat16),
            preferred_element_type=jnp.float32,
        )
        product = product + jnp.einsum(
            "qlh,lhy->qly",
            distant_panels,
            off_block.astype(jnp.bfloat16),
            preferred_element_type=jnp.float32,
        )
        squares = jnp.sum(product * product)
        local_terms = -jnp.sum(jnp.log(diag_values)) + penalty * (
            jnp.sum(jnp.abs(diag_block)) + jnp.sum(jnp.abs(off_block))
        )
        part_value = (squares / (2.0 * total_rows) + samp_first * local_terms) / matrix_order
        objective_parts.append(part_value)
        lower_precision_product = product.astype(jnp.bfloat16)
        grad_diag = jnp.einsum(
            "rei,reo->eio",
            nearby_panels,
            lower_precision_product,
            preferred_element_type=jnp.float32,
        )
        grad_off = jnp.einsum(
            "rei,reo->eio",
            distant_panels,
            lower_precision_product,
            preferred_element_type=jnp.float32,
        )
        grad_diag, grad_off = lax.psum((grad_diag, grad_off), "samp")
        diag_block, off_block, diag_values = advance(
            diag_block, off_block, diag_values, grad_diag, grad_off, diag_mask, total_rows
        )
    objective = lax.psum(jnp.stack(objective_parts), ("samp", "var"))
    new_blocks = jnp.where(flags, diag_block[:, None], off_block[:, None])
    return (new_blocks, diag_values.reshape(-1), objective)


def power_of_two(count):
    return count & (count - 1) == 0


def whole_body(observed, blocks, diagonal, pattern):
    cols = blocks.shape[0]
    var, samp = lax.axis_size("var"), lax.axis_size("samp")
    exact = samp * var == cols and cols % 4 == 0 and var % 8 == 0 and blocks.shape[2] == 128
    if exact and power_of_two(samp) and power_of_two(var):
        return column_body(observed, blocks, diagonal, pattern)
    return body(observed, blocks, diagonal, pattern)


def solution(mesh):
    placed = (P("samp", "var"), P("var", None, None, None), P("var"), P("var", None))
    return jax.shard_map(
        whole_body,
        mesh=mesh,
        in_specs=placed,
        out_specs=(P("var", None, None, None), P("var"), P()),
        check_vma=False,
    )
```

```python
import functools

import jax
import jax.numpy as jnp
from jax import lax
from jax.experimental import pallas as pl
from jax.experimental.pallas import tpu as pltpu
from jax.sharding import PartitionSpec as P

STEPS = 2


step_length = 0.5
penalty = 0.5
MESH = pl.DeviceIdType.MESH


def shrink(moved, level):
    return moved - jnp.clip(moved, -level, level)


def flip(index, offset, count):
    out, bit = 0, 1
    while bit < count:
        out = out + ((index // bit + offset // bit) % 2) * bit
        bit *= 2
    return out


def main_kernel(samp, var, near_idx, wanted, own_slot, want_ref, x_hbm, blk_hbm, dia_ref,
                fin_ref, tails_ref, obj_ref,
                x, blk, ask, ask_s, far, farz, cc_out, cc_in, cc_own, oo_out, oo_in, oo_own, oz, acc,
                load, ask_ss, ask_rs, ask_l, cc_s, cc_r, z_s, z_r, oo_s, oo_r, out_s, out_r,
                rel_s, rel_r, tail_s, tail_r, oz_s, oz_r):
    s = lax.axis_index("samp")
    v = lax.axis_index("var")
    rows, width = x.shape[1], x.shape[2]
    total_rows = rows * samp
    over_first = (((0,), (0,)), ((), ()))

    cols = x.shape[0]
    x_loads = [
        pltpu.make_async_copy(x_hbm.at[:, l * width:(l + 1) * width], x.at[l], load.at[l])
        for l in range(cols)
    ]
    for x_load in x_loads:
        x_load.start()
    blk_load = pltpu.make_async_copy(blk_hbm, blk, load.at[cols])
    blk_load.start()

    barrier = pltpu.get_barrier_semaphore()
    for i in range(1, var):
        pl.semaphore_signal(barrier, inc=1, device_id={"var": flip(v, i, var)}, device_id_type=MESH)
    for d in range(1, samp):
        pl.semaphore_signal(barrier, inc=1, device_id={"samp": flip(s, d, samp)}, device_id_type=MESH)
    pl.semaphore_wait(barrier, samp + var - 2)

    def remote(src, dst, send, recv, **where):
        return pltpu.make_async_remote_copy(
            src_ref=src, dst_ref=dst, send_sem=send, recv_sem=recv,
            device_id=where, device_id_type=MESH)

    def ask_copy(i):
        u = flip(v, i, var)
        return remote(want_ref.at[u], ask.at[v], ask_ss.at[i], ask_rs.at[i], var=u)

    def z_copy(i):
        u = flip(v, i, var)
        return remote(far.at[u], farz.at[v], z_s.at[i], z_r.at[i], var=u)

    def cc_copy(d, i):
        u, k = flip(v, i, var), flip(s, d, samp)
        return remote(cc_out.at[u, k], cc_in.at[u, s], cc_s.at[d, i], cc_r.at[d, i], samp=k)

    def oo_copy(d, i):
        u, k = flip(v, i, var), flip(s, d, samp)
        return remote(oo_out.at[u, k], oo_in.at[u, s], oo_s.at[d, i], oo_r.at[d, i], samp=k)

    def out_copy(d, i):
        u, k = flip(v, i, var), flip(s, d, samp)
        return remote(fin_ref.at[s, u], fin_ref.at[s, u], out_s.at[d, i], out_r.at[d, i], samp=k)

    def panel(index):
        return x[index]

    def near_panel(u, k):
        return panel(near_idx[u * samp + k])

    def gram(left, right):
        return lax.dot_general(left, right, over_first, preferred_element_type=jnp.float32)

    eye = lax.broadcasted_iota(jnp.int32, (width, width), 0) == lax.broadcasted_iota(
        jnp.int32, (width, width), 1)

    row_at = lax.broadcasted_iota(jnp.int32, (width, width), 0)
    col_at = lax.broadcasted_iota(jnp.int32, (width, width), 1)
    spare = (row_at == col_at + 1) | ((row_at == width - 1) & (col_at == 0))

    def rounded_symmetric(part):
        off = jnp.where(eye, part - part.astype(jnp.bfloat16).astype(jnp.float32), 0.0)
        row = jnp.sum(off, axis=0, keepdims=True)
        below = jnp.where(row_at == col_at + 1, row, part)
        corner = jnp.where((row_at == width - 1) & (col_at == 0), row[:, width - 1:], below)
        return corner.astype(jnp.bfloat16)

    def own_symmetric(part):
        return jnp.where(spare, 0.0, part)

    def restored(total):
        below = jnp.where(row_at == col_at + 1, total, 0.0)
        row = jnp.sum(below, axis=0, keepdims=True)
        last = total[width - 1:, :1]
        row = jnp.where(col_at[:1] == width - 1, last, row)
        return jnp.where(spare, total.T, total) + jnp.where(eye, row, 0.0)

    def start_cc(i):
        u = flip(v, i, var)
        for d in range(samp):
            k = flip(s, d, samp)
            c = near_panel(u, k)
            part = gram(c, c)
            if d == 0:
                cc_own[u] = own_symmetric(part)
            else:
                cc_out[u, k] = rounded_symmetric(part)
                cc_copy(d, i).start()

    def start_oo(i, far_panel):
        u = flip(v, i, var)
        for d in range(samp):
            k = flip(s, d, samp)
            o = far_panel(u, k)
            part = gram(o, jnp.concatenate([near_panel(u, k), o], axis=1))
            if d == 0:
                oo_own[u, :, :width] = part[:, :width]
                oo_own[u, :, width:] = own_symmetric(part[:, width:])
            else:
                oo_out[u, k, :, :width] = part[:, :width].astype(jnp.bfloat16)
                oo_out[u, k, :, width:] = rounded_symmetric(part[:, width:])
                oo_copy(d, i).start()

    def column(i):
        u = flip(v, i, var)
        for d in range(1, samp):
            cc_copy(d, i).wait_recv()
            oo_copy(d, i).wait_recv()
        cc, oc, oo = cc_own[u], oo_own[u, :, :width], oo_own[u, :, width:]
        for d in range(1, samp):
            p = flip(s, d, samp)
            cc = cc + cc_in[u, p].astype(jnp.float32)
            oc = oc + oo_in[u, p, :, :width].astype(jnp.float32)
            oo = oo + oo_in[u, p, :, width:].astype(jnp.float32)
        cc, oo = restored(cc), restored(oo)
        both = jnp.concatenate(
            [jnp.concatenate([cc, oc.T], axis=1), jnp.concatenate([oc, oo], axis=1)], axis=0)
        high = both.astype(jnp.bfloat16)
        low = (both - high.astype(jnp.float32)).astype(jnp.bfloat16)
        gram_parts = jnp.concatenate([high, low], axis=1)
        col = near_idx[u * samp + s]
        slot = own_slot[u * samp + s]
        wd = jnp.where(eye, 0.0, blk[col, slot])
        wo = blk[col, 1 - slot]
        dv = dia_ref[col]
        for step in range(STEPS):
            rounded = jnp.concatenate(
                [jnp.where(eye, dv, wd).astype(jnp.bfloat16), wo.astype(jnp.bfloat16)], axis=0)
            grad = jnp.dot(gram_parts, jnp.concatenate([rounded, rounded], axis=0),
                           preferred_element_type=jnp.float32)
            squares = jnp.sum(grad * rounded.astype(jnp.float32), axis=0, keepdims=True)
            terms = (squares / (2.0 * total_rows) - jnp.log(dv)
                     + penalty * jnp.sum(jnp.abs(wd) + jnp.abs(wo), axis=0, keepdims=True))
            acc[step:step + 1, :] += terms
            grad = grad / total_rows
            gd, go = grad[:width], grad[width:]
            wo = shrink(wo - step_length * go, step_length * penalty)
            wd = jnp.where(eye, 0.0, shrink(wd - step_length * gd, step_length * penalty))
            along = jnp.sum(jnp.where(eye, gd, 0.0), axis=0, keepdims=True)
            moved = dv - step_length * along
            dv = 0.5 * (moved + jnp.sqrt(moved * moved + 4.0 * step_length))
        fin_ref[s, u, 0] = wd.astype(jnp.bfloat16)
        fin_ref[s, u, 1] = wo.astype(jnp.bfloat16)
        tails_ref[s, pl.ds(u, 1), :] = dv

    def send_out(i, direct):
        for d in range(1, samp if direct else samp - 1):
            out_copy(d, i).start()

    def relay_copy(part, i):
        u = flip(v, i, var)
        near, to = flip(s, 1 + part, samp), flip(s, 2 - part, samp)
        return remote(fin_ref.at[near, u, part], fin_ref.at[near, u, part],
                      rel_s.at[part, i], rel_r.at[part, i], samp=to)

    def relay(i):
        for part in range(2):
            out_copy(1 + part, i).wait_recv()
            relay_copy(part, i).start()

    for i in range(1, var):
        ask_copy(i).start()
    acc[...] = jnp.zeros_like(acc)
    for x_load in x_loads:
        x_load.wait()
    start_cc(0)
    for i in range(1, var):
        ask_copy(i).wait_recv()
    ask[v] = want_ref[v]
    ask_load = pltpu.make_async_copy(ask, ask_s, ask_l)
    ask_load.start()
    ask_load.wait()

    def send_far(i, carry):
        u = flip(v, i, var)
        for k in range(samp):
            far[u, k] = panel(ask_s[u, 0, k])
        z_copy(i).start()
        return carry

    lax.fori_loop(1, var, send_far, 0)
    start_oo(0, lambda u, k: panel(wanted[u * samp + k]))
    lax.fori_loop(1, var, lambda i, c: (start_cc(i), c)[1], 0)
    blk_load.wait()

    def turn(i, carry):
        @pl.when(i < var)
        def _():
            z_copy(i).wait_recv()
            start_oo(i, lambda u, k: farz[u, k])

        column(i - 1)

        @pl.when(i < var - 1)
        def _():
            send_out(i - 1, False)

        @pl.when(i == var - 1)
        def _():
            send_out(i - 1, True)

        @pl.when(i > 2)
        def _():
            relay(i - 3)

        return carry

    lax.fori_loop(1, var + 1, turn, 0)

    tails_ref[s, var:, :] = acc[...]

    def tail_copy(d):
        return remote(tails_ref.at[s], tails_ref.at[s], tail_s.at[d], tail_r.at[d],
                      samp=flip(s, d, samp))

    def oz_copy(i):
        return remote(oz.at[v], oz.at[v], oz_s.at[i], oz_r.at[i], var=flip(v, i, var))

    for d in range(1, samp):
        tail_copy(d).start()
    send_out(var - 1, True)
    for d in range(1, samp):
        tail_copy(d).wait_recv()
    group = tails_ref[0, var:, :]
    for k in range(1, samp):
        group = group + tails_ref[k, var:, :]
    oz[v] = group
    for i in range(1, var):
        oz_copy(i).start()
    for i in range(1, var):
        oz_copy(i).wait_recv()
    whole = oz[0]
    for u in range(1, var):
        whole = whole + oz[u]
    obj_ref[...] = whole

    def finish(i, carry):
        for d in range(1, samp):
            cc_copy(d, i).wait_send()
            oo_copy(d, i).wait_send()
        for d in range(1, samp - 1):
            out_copy(d, i).wait_send()
        return carry

    def finish_relay(i, carry):
        for part in range(2):
            relay_copy(part, i).wait()
        return carry

    lax.fori_loop(0, var, finish, 0)
    lax.fori_loop(0, var - 2, finish_relay, 0)
    for i in range(var - 2, var):
        for d in range(1, samp - 1):
            out_copy(d, i).wait_recv()
        out_copy(samp - 1, i).wait()
    for d in range(1, samp):
        tail_copy(d).wait_send()
    for i in range(1, var):
        ask_copy(i).wait_send()
        z_copy(i).wait_send()
        oz_copy(i).wait_send()


def unpack_kernel(group, order, owner, rank, slot, fin_ref, tails_ref, whole_ref, out_ref, dia_ref, obj_ref):
    @pl.when(pl.program_id(0) == 0)
    def _():
        for step in range(STEPS):
            obj_ref[step] = jnp.sum(whole_ref[step:step + 1, :]) / order

    first = pl.program_id(0) * group
    for j in range(group):
        col = first + j
        k, u, at = rank[col], owner[col], slot[col]
        out_ref[j, 0] = fin_ref[k, u, at].astype(jnp.float32)
        out_ref[j, 1] = fin_ref[k, u, 1 - at].astype(jnp.float32)
        dia_ref[pl.ds(col, 1), :] = tails_ref[k, pl.ds(u, 1), :]


def column_body(observed, blocks, diagonal, pattern):
    cols, width = blocks.shape[0], blocks.shape[2]
    rows = observed.shape[0]
    var, samp = lax.axis_size("var"), lax.axis_size("samp")
    v = lax.axis_index("var")
    ids = jnp.arange(cols, dtype=jnp.int32)
    on_diag = pattern == (v * cols + ids)[:, None]
    off_row = jnp.sum(jnp.where(on_diag, 0, pattern), axis=1)
    diag_slot = jnp.where(on_diag[:, 1], 1, 0).astype(jnp.int32)
    owner = off_row // cols
    resident = off_row % cols
    earlier = (owner[None, :] == owner[:, None]) & (ids[None, :] < ids[:, None])
    rank = jnp.sum(earlier, axis=1).astype(jnp.int32)
    slot_index = owner * samp + rank
    match = slot_index[:, None] == ids[None, :]
    wanted = jnp.sum(jnp.where(match, resident[:, None], 0), axis=0)
    near_idx = jnp.sum(jnp.where(match, ids[:, None], 0), axis=0)
    own_slot = jnp.sum(jnp.where(match, diag_slot[:, None], 0), axis=0)
    want = jnp.pad(wanted.reshape(var, 1, samp), ((0, 0), (0, 0), (0, width - samp)))

    vmem = pl.BlockSpec(memory_space=pltpu.VMEM)
    smem = pl.BlockSpec(memory_space=pltpu.SMEM)
    hbm = pl.BlockSpec(memory_space=pl.ANY)
    dma = pltpu.SemaphoreType.DMA
    bf16, f32 = jnp.bfloat16, jnp.float32
    fin, tails, whole = pl.pallas_call(
        functools.partial(main_kernel, samp, var),
        out_shape=(
            jax.ShapeDtypeStruct((samp, var, 2, width, width), bf16),
            jax.ShapeDtypeStruct((samp, var + 8, width), f32),
            jax.ShapeDtypeStruct((8, width), f32),
        ),
        in_specs=[smem, smem, smem, vmem, hbm, hbm, vmem],
        out_specs=(vmem,) * 3,
        scratch_shapes=[
            pltpu.VMEM((cols, rows, width), observed.dtype),
            pltpu.VMEM(blocks.shape, f32),
            pltpu.VMEM((var, 1, width), jnp.int32),
            pltpu.SMEM((var, 1, width), jnp.int32),
            pltpu.VMEM((var, samp, rows, width), observed.dtype),
            pltpu.VMEM((var, samp, rows, width), observed.dtype),
            pltpu.VMEM((var, samp, width, width), bf16),
            pltpu.VMEM((var, samp, width, width), bf16),
            pltpu.VMEM((var, width, width), f32),
            pltpu.VMEM((var, samp, width, 2 * width), bf16),
            pltpu.VMEM((var, samp, width, 2 * width), bf16),
            pltpu.VMEM((var, width, 2 * width), f32),
            pltpu.VMEM((var, 8, width), f32),
            pltpu.VMEM((8, width), f32),
            dma((cols + 1,)), dma((var,)), dma((var,)), dma,
            dma((samp, var)), dma((samp, var)), dma((var,)), dma((var,)),
            dma((samp, var)), dma((samp, var)), dma((samp, var)), dma((samp, var)),
            dma((2, var)), dma((2, var)), dma((samp,)), dma((samp,)), dma((var,)), dma((var,)),
        ],
        compiler_params=pltpu.CompilerParams(collective_id=0, has_side_effects=True),
        name="columns",
    )(near_idx, wanted, own_slot, want, observed, blocks, diagonal.reshape(cols, 1, width))

    group = 4
    new_blocks, new_diagonal, objective = pl.pallas_call(
        functools.partial(unpack_kernel, group, float(cols * width * var)),
        out_shape=(
            jax.ShapeDtypeStruct(blocks.shape, jnp.float32),
            jax.ShapeDtypeStruct((cols, width), jnp.float32),
            jax.ShapeDtypeStruct((STEPS,), jnp.float32),
        ),
        grid=(cols // group,),
        in_specs=[smem, smem, smem, vmem, vmem, vmem],
        out_specs=(
            pl.BlockSpec((group, 2, width, width), lambda g: (g, 0, 0, 0)),
            pl.BlockSpec((cols, width), lambda g: (0, 0)),
            smem,
        ),
        name="unpack",
    )(owner, rank, diag_slot, fin, tails, whole)
    return new_blocks, new_diagonal.reshape(-1), objective


def advance(diag_block, off_block, diag_values, grad_diag, grad_off, diag_mask, total_rows):
    grad_diag = grad_diag / total_rows
    grad_off = grad_off / total_rows
    new_off = shrink(off_block - step_length * grad_off, step_length * penalty)
    new_diag_block = jnp.where(
        diag_mask, 0.0, shrink(diag_block - step_length * grad_diag, step_length * penalty)
    )
    along = jnp.sum(jnp.where(diag_mask, grad_diag, 0.0), axis=1)
    moved = diag_values - step_length * along
    new_values = 0.5 * (moved + jnp.sqrt(moved * moved + 4.0 * step_length))
    return (new_diag_block, new_off, new_values)


def body(observed, blocks, diagonal, pattern):
    col_count = blocks.shape[0]
    block_width = blocks.shape[2]
    sample_rows = observed.shape[0]
    var_count = lax.axis_size("var")
    samp_count = lax.axis_size("samp")
    capacity = max(2, -(-col_count // var_count))
    total_rows = sample_rows * samp_count
    matrix_order = col_count * block_width * var_count
    var_index = lax.axis_index("var")
    column_ids = jnp.arange(col_count, dtype=jnp.int32)
    columns = var_index * col_count + column_ids
    on_diag = pattern == columns[:, None]
    off_row = jnp.sum(jnp.where(on_diag, 0, pattern), axis=1)
    owner_index = off_row // col_count
    resident_block = off_row % col_count
    earlier = (owner_index[None, :] == owner_index[:, None]) & (
        column_ids[None, :] < column_ids[:, None]
    )
    position_rank = jnp.sum(earlier, axis=1)
    slot_index = owner_index * capacity + position_rank
    all_slots = jnp.arange(var_count * capacity, dtype=jnp.int32)
    slot_match = slot_index[:, None] == all_slots[None, :]
    wanted = jnp.sum(jnp.where(slot_match, resident_block[:, None], 0), axis=0)
    asked_blocks = lax.all_to_all(wanted, "var", split_axis=0, concat_axis=0, tiled=True)
    nearby_panels = observed.reshape(sample_rows, col_count, block_width)
    outgoing = jnp.take(nearby_panels, asked_blocks, axis=1)
    arrived = lax.all_to_all(outgoing, "var", split_axis=1, concat_axis=1, tiled=True)
    distant_panels = jnp.take(arrived, slot_index, axis=1)
    diag_mask = jnp.eye(block_width, dtype=bool)
    flags = on_diag[:, :, None, None]
    diag_block = jnp.sum(jnp.where(flags, blocks, 0.0), axis=1)
    diag_block = jnp.where(diag_mask, 0.0, diag_block)
    off_block = jnp.sum(jnp.where(flags, 0.0, blocks), axis=1)
    diag_values = diagonal.reshape(col_count, block_width)
    samp_first = (lax.axis_index("samp") == 0).astype(jnp.float32)
    objective_parts = []
    for iteration in range(STEPS):
        full_diag = jnp.where(diag_mask, diag_values[:, None, :], diag_block)
        product = jnp.einsum(
            "qlh,lhy->qly",
            nearby_panels,
            full_diag.astype(jnp.bfloat16),
            preferred_element_type=jnp.float32,
        )
        product = product + jnp.einsum(
            "qlh,lhy->qly",
            distant_panels,
            off_block.astype(jnp.bfloat16),
            preferred_element_type=jnp.float32,
        )
        squares = jnp.sum(product * product)
        local_terms = -jnp.sum(jnp.log(diag_values)) + penalty * (
            jnp.sum(jnp.abs(diag_block)) + jnp.sum(jnp.abs(off_block))
        )
        part_value = (squares / (2.0 * total_rows) + samp_first * local_terms) / matrix_order
        objective_parts.append(part_value)
        lower_precision_product = product.astype(jnp.bfloat16)
        grad_diag = jnp.einsum(
            "rei,reo->eio",
            nearby_panels,
            lower_precision_product,
            preferred_element_type=jnp.float32,
        )
        grad_off = jnp.einsum(
            "rei,reo->eio",
            distant_panels,
            lower_precision_product,
            preferred_element_type=jnp.float32,
        )
        grad_diag, grad_off = lax.psum((grad_diag, grad_off), "samp")
        diag_block, off_block, diag_values = advance(
            diag_block, off_block, diag_values, grad_diag, grad_off, diag_mask, total_rows
        )
    objective = lax.psum(jnp.stack(objective_parts), ("samp", "var"))
    new_blocks = jnp.where(flags, diag_block[:, None], off_block[:, None])
    return (new_blocks, diag_values.reshape(-1), objective)


def power_of_two(count):
    return count & (count - 1) == 0


def whole_body(observed, blocks, diagonal, pattern):
    cols = blocks.shape[0]
    var, samp = lax.axis_size("var"), lax.axis_size("samp")
    exact = samp == 4 and samp * var == cols and cols % 4 == 0 and var % 8 == 0 and blocks.shape[2] == 128
    if exact and power_of_two(samp) and power_of_two(var):
        return column_body(observed, blocks, diagonal, pattern)
    return body(observed, blocks, diagonal, pattern)


def solution(mesh):
    placed = (P("samp", "var"), P("var", None, None, None), P("var"), P("var", None))
    return jax.shard_map(
        whole_body,
        mesh=mesh,
        in_specs=placed,
        out_specs=(P("var", None, None, None), P("var"), P()),
        check_vma=False,
    )
```

```python
import functools

import jax
import jax.numpy as jnp
from jax import lax
from jax.experimental import pallas as pl
from jax.experimental.pallas import tpu as pltpu
from jax.sharding import PartitionSpec as P

STEPS = 2


step_length = 0.5
penalty = 0.5
MESH = pl.DeviceIdType.MESH


def shrink(moved, level):
    return moved - jnp.clip(moved, -level, level)


def flip(index, offset, count):
    out, bit = 0, 1
    while bit < count:
        out = out + ((index // bit + offset // bit) % 2) * bit
        bit *= 2
    return out


def main_kernel(samp, var, near_idx, wanted, own_slot, want_ref, x_hbm, blk_hbm, dia_ref,
                fin_ref, tails_ref, obj_ref,
                x, blk, ask, ask_s, far, farz, cc_out, cc_in, cc_own, oo_out, oo_in, oo_own, oz, acc,
                load, ask_ss, ask_rs, ask_l, cc_s, cc_r, z_s, z_r, oo_s, oo_r, out_s, out_r,
                rel_s, rel_r, tail_s, tail_r, oz_s, oz_r):
    s = lax.axis_index("samp")
    v = lax.axis_index("var")
    rows, width = x.shape[1], x.shape[2]
    total_rows = rows * samp
    over_first = (((0,), (0,)), ((), ()))

    cols = x.shape[0]
    x_loads = [
        pltpu.make_async_copy(x_hbm.at[:, l * width:(l + 1) * width], x.at[l], load.at[l])
        for l in range(cols)
    ]
    for x_load in x_loads:
        x_load.start()
    blk_load = pltpu.make_async_copy(blk_hbm, blk, load.at[cols])
    blk_load.start()

    barrier = pltpu.get_barrier_semaphore()
    for i in range(1, var):
        pl.semaphore_signal(barrier, inc=1, device_id={"var": flip(v, i, var)}, device_id_type=MESH)
    for d in range(1, samp):
        pl.semaphore_signal(barrier, inc=1, device_id={"samp": flip(s, d, samp)}, device_id_type=MESH)
    pl.semaphore_wait(barrier, samp + var - 2)

    def remote(src, dst, send, recv, **where):
        return pltpu.make_async_remote_copy(
            src_ref=src, dst_ref=dst, send_sem=send, recv_sem=recv,
            device_id=where, device_id_type=MESH)

    def ask_copy(i):
        u = flip(v, i, var)
        return remote(want_ref.at[u], ask.at[v], ask_ss.at[i], ask_rs.at[i], var=u)

    def z_copy(i):
        u = flip(v, i, var)
        return remote(far.at[u], farz.at[v], z_s.at[i], z_r.at[i], var=u)

    def cc_copy(d, i):
        u, k = flip(v, i, var), flip(s, d, samp)
        return remote(cc_out.at[u, k], cc_in.at[u, s], cc_s.at[d, i], cc_r.at[d, i], samp=k)

    def oo_copy(d, i):
        u, k = flip(v, i, var), flip(s, d, samp)
        return remote(oo_out.at[u, k], oo_in.at[u, s], oo_s.at[d, i], oo_r.at[d, i], samp=k)

    def out_copy(d, i):
        u, k = flip(v, i, var), flip(s, d, samp)
        return remote(fin_ref.at[s, u], fin_ref.at[s, u], out_s.at[d, i], out_r.at[d, i], samp=k)

    def panel(index):
        return x[index]

    def near_panel(u, k):
        return panel(near_idx[u * samp + k])

    def gram(left, right):
        return lax.dot_general(left, right, over_first, preferred_element_type=jnp.float32)

    eye = lax.broadcasted_iota(jnp.int32, (width, width), 0) == lax.broadcasted_iota(
        jnp.int32, (width, width), 1)

    row_at = lax.broadcasted_iota(jnp.int32, (width, width), 0)
    col_at = lax.broadcasted_iota(jnp.int32, (width, width), 1)
    spare = (row_at == col_at + 1) | ((row_at == width - 1) & (col_at == 0))

    def rounded_symmetric(part):
        off = jnp.where(eye, part - part.astype(jnp.bfloat16).astype(jnp.float32), 0.0)
        row = jnp.sum(off, axis=0, keepdims=True)
        below = jnp.where(row_at == col_at + 1, row, part)
        corner = jnp.where((row_at == width - 1) & (col_at == 0), row[:, width - 1:], below)
        return corner.astype(jnp.bfloat16)

    def own_symmetric(part):
        return jnp.where(spare, 0.0, part)

    def restored(total):
        below = jnp.where(row_at == col_at + 1, total, 0.0)
        row = jnp.sum(below, axis=0, keepdims=True)
        last = total[width - 1:, :1]
        row = jnp.where(col_at[:1] == width - 1, last, row)
        return jnp.where(spare, total.T, total) + jnp.where(eye, row, 0.0)

    def start_cc(i):
        u = flip(v, i, var)
        for d in range(samp):
            k = flip(s, d, samp)
            c = near_panel(u, k)
            part = gram(c, c)
            if d == 0:
                cc_own[u] = own_symmetric(part)
            else:
                cc_out[u, k] = rounded_symmetric(part)
                cc_copy(d, i).start()

    def start_oo(i, far_panel):
        u = flip(v, i, var)
        for d in range(samp):
            k = flip(s, d, samp)
            o = far_panel(u, k)
            part = gram(o, jnp.concatenate([near_panel(u, k), o], axis=1))
            if d == 0:
                oo_own[u, :, :width] = part[:, :width]
                oo_own[u, :, width:] = own_symmetric(part[:, width:])
            else:
                oo_out[u, k, :, :width] = part[:, :width].astype(jnp.bfloat16)
                oo_out[u, k, :, width:] = rounded_symmetric(part[:, width:])
                oo_copy(d, i).start()

    def column(i):
        u = flip(v, i, var)
        for d in range(1, samp):
            cc_copy(d, i).wait_recv()
            oo_copy(d, i).wait_recv()
        cc, oc, oo = cc_own[u], oo_own[u, :, :width], oo_own[u, :, width:]
        for d in range(1, samp):
            p = flip(s, d, samp)
            cc = cc + cc_in[u, p].astype(jnp.float32)
            oc = oc + oo_in[u, p, :, :width].astype(jnp.float32)
            oo = oo + oo_in[u, p, :, width:].astype(jnp.float32)
        cc, oo = restored(cc), restored(oo)
        both = jnp.concatenate(
            [jnp.concatenate([cc, oc.T], axis=1), jnp.concatenate([oc, oo], axis=1)], axis=0)
        high = both.astype(jnp.bfloat16)
        low = (both - high.astype(jnp.float32)).astype(jnp.bfloat16)
        gram_parts = jnp.concatenate([high, low], axis=1)
        col = near_idx[u * samp + s]
        slot = own_slot[u * samp + s]
        wd = jnp.where(eye, 0.0, blk[col, slot])
        wo = blk[col, 1 - slot]
        dv = dia_ref[col]
        for step in range(STEPS):
            rounded = jnp.concatenate(
                [jnp.where(eye, dv, wd).astype(jnp.bfloat16), wo.astype(jnp.bfloat16)], axis=0)
            grad = jnp.dot(gram_parts, jnp.concatenate([rounded, rounded], axis=0),
                           preferred_element_type=jnp.float32)
            squares = jnp.sum(grad * rounded.astype(jnp.float32), axis=0, keepdims=True)
            terms = (squares / (2.0 * total_rows) - jnp.log(dv)
                     + penalty * jnp.sum(jnp.abs(wd) + jnp.abs(wo), axis=0, keepdims=True))
            acc[step:step + 1, :] += terms
            grad = grad / total_rows
            gd, go = grad[:width], grad[width:]
            wo = shrink(wo - step_length * go, step_length * penalty)
            wd = jnp.where(eye, 0.0, shrink(wd - step_length * gd, step_length * penalty))
            along = jnp.sum(jnp.where(eye, gd, 0.0), axis=0, keepdims=True)
            moved = dv - step_length * along
            dv = 0.5 * (moved + jnp.sqrt(moved * moved + 4.0 * step_length))
        fin_ref[s, u, 0] = wd.astype(jnp.bfloat16)
        fin_ref[s, u, 1] = wo.astype(jnp.bfloat16)
        tails_ref[s, pl.ds(u, 1), :] = dv

    def send_out(i, direct):
        for d in range(1, samp if direct else samp - 1):
            out_copy(d, i).start()

    def relay_copy(part, i):
        u = flip(v, i, var)
        near, to = flip(s, 1 + part, samp), flip(s, 2 - part, samp)
        return remote(fin_ref.at[near, u, part], fin_ref.at[near, u, part],
                      rel_s.at[part, i], rel_r.at[part, i], samp=to)

    def relay(i):
        for part in range(2):
            out_copy(1 + part, i).wait_recv()
            relay_copy(part, i).start()

    for i in range(1, var):
        ask_copy(i).start()
    acc[...] = jnp.zeros_like(acc)
    for x_load in x_loads:
        x_load.wait()
    start_cc(0)
    for i in range(1, var):
        ask_copy(i).wait_recv()
    ask[v] = want_ref[v]
    ask_load = pltpu.make_async_copy(ask, ask_s, ask_l)
    ask_load.start()
    ask_load.wait()

    def send_far(i, carry):
        u = flip(v, i, var)
        for k in range(samp):
            far[u, k] = panel(ask_s[u, 0, k])
        z_copy(i).start()
        return carry

    lax.fori_loop(1, var, send_far, 0)
    start_oo(0, lambda u, k: panel(wanted[u * samp + k]))
    lax.fori_loop(1, var, lambda i, c: (start_cc(i), c)[1], 0)
    blk_load.wait()

    def take_far(i):
        z_copy(i).wait_recv()
        start_oo(i, lambda u, k: farz[u, k])

    def turn(i, carry):
        @pl.when(i <= var // 2)
        def _():
            take_far(i)

        column(i - 1)

        @pl.when(i < var - 1)
        def _():
            send_out(i - 1, False)

        @pl.when(i == var - 1)
        def _():
            send_out(i - 1, True)

        @pl.when(i > 2)
        def _():
            relay(i - 3)

        @pl.when((i > var // 2) & (i < var))
        def _():
            take_far(i)

        return carry

    lax.fori_loop(1, var + 1, turn, 0)

    tails_ref[s, var:, :] = acc[...]

    def tail_copy(d):
        return remote(tails_ref.at[s], tails_ref.at[s], tail_s.at[d], tail_r.at[d],
                      samp=flip(s, d, samp))

    def oz_copy(i):
        return remote(oz.at[v], oz.at[v], oz_s.at[i], oz_r.at[i], var=flip(v, i, var))

    for d in range(1, samp):
        tail_copy(d).start()
    send_out(var - 1, True)
    for d in range(1, samp):
        tail_copy(d).wait_recv()
    group = tails_ref[0, var:, :]
    for k in range(1, samp):
        group = group + tails_ref[k, var:, :]
    oz[v] = group
    for i in range(1, var):
        oz_copy(i).start()
    for i in range(1, var):
        oz_copy(i).wait_recv()
    whole = oz[0]
    for u in range(1, var):
        whole = whole + oz[u]
    obj_ref[...] = whole

    def finish(i, carry):
        for d in range(1, samp):
            cc_copy(d, i).wait_send()
            oo_copy(d, i).wait_send()
        for d in range(1, samp - 1):
            out_copy(d, i).wait_send()
        return carry

    def finish_relay(i, carry):
        for part in range(2):
            relay_copy(part, i).wait()
        return carry

    lax.fori_loop(0, var, finish, 0)
    lax.fori_loop(0, var - 2, finish_relay, 0)
    for i in range(var - 2, var):
        for d in range(1, samp - 1):
            out_copy(d, i).wait_recv()
        out_copy(samp - 1, i).wait()
    for d in range(1, samp):
        tail_copy(d).wait_send()
    for i in range(1, var):
        ask_copy(i).wait_send()
        z_copy(i).wait_send()
        oz_copy(i).wait_send()


def unpack_kernel(group, order, owner, rank, slot, fin_ref, tails_ref, whole_ref, out_ref, dia_ref, obj_ref):
    @pl.when(pl.program_id(0) == 0)
    def _():
        for step in range(STEPS):
            obj_ref[step] = jnp.sum(whole_ref[step:step + 1, :]) / order

    first = pl.program_id(0) * group
    for j in range(group):
        col = first + j
        k, u, at = rank[col], owner[col], slot[col]
        out_ref[j, 0] = fin_ref[k, u, at].astype(jnp.float32)
        out_ref[j, 1] = fin_ref[k, u, 1 - at].astype(jnp.float32)
        dia_ref[pl.ds(col, 1), :] = tails_ref[k, pl.ds(u, 1), :]


def column_body(observed, blocks, diagonal, pattern):
    cols, width = blocks.shape[0], blocks.shape[2]
    rows = observed.shape[0]
    var, samp = lax.axis_size("var"), lax.axis_size("samp")
    v = lax.axis_index("var")
    ids = jnp.arange(cols, dtype=jnp.int32)
    on_diag = pattern == (v * cols + ids)[:, None]
    off_row = jnp.sum(jnp.where(on_diag, 0, pattern), axis=1)
    diag_slot = jnp.where(on_diag[:, 1], 1, 0).astype(jnp.int32)
    owner = off_row // cols
    resident = off_row % cols
    earlier = (owner[None, :] == owner[:, None]) & (ids[None, :] < ids[:, None])
    rank = jnp.sum(earlier, axis=1).astype(jnp.int32)
    slot_index = owner * samp + rank
    match = slot_index[:, None] == ids[None, :]
    wanted = jnp.sum(jnp.where(match, resident[:, None], 0), axis=0)
    near_idx = jnp.sum(jnp.where(match, ids[:, None], 0), axis=0)
    own_slot = jnp.sum(jnp.where(match, diag_slot[:, None], 0), axis=0)
    want = jnp.pad(wanted.reshape(var, 1, samp), ((0, 0), (0, 0), (0, width - samp)))

    vmem = pl.BlockSpec(memory_space=pltpu.VMEM)
    smem = pl.BlockSpec(memory_space=pltpu.SMEM)
    hbm = pl.BlockSpec(memory_space=pl.ANY)
    dma = pltpu.SemaphoreType.DMA
    bf16, f32 = jnp.bfloat16, jnp.float32
    fin, tails, whole = pl.pallas_call(
        functools.partial(main_kernel, samp, var),
        out_shape=(
            jax.ShapeDtypeStruct((samp, var, 2, width, width), bf16),
            jax.ShapeDtypeStruct((samp, var + 8, width), f32),
            jax.ShapeDtypeStruct((8, width), f32),
        ),
        in_specs=[smem, smem, smem, vmem, hbm, hbm, vmem],
        out_specs=(vmem,) * 3,
        scratch_shapes=[
            pltpu.VMEM((cols, rows, width), observed.dtype),
            pltpu.VMEM(blocks.shape, f32),
            pltpu.VMEM((var, 1, width), jnp.int32),
            pltpu.SMEM((var, 1, width), jnp.int32),
            pltpu.VMEM((var, samp, rows, width), observed.dtype),
            pltpu.VMEM((var, samp, rows, width), observed.dtype),
            pltpu.VMEM((var, samp, width, width), bf16),
            pltpu.VMEM((var, samp, width, width), bf16),
            pltpu.VMEM((var, width, width), f32),
            pltpu.VMEM((var, samp, width, 2 * width), bf16),
            pltpu.VMEM((var, samp, width, 2 * width), bf16),
            pltpu.VMEM((var, width, 2 * width), f32),
            pltpu.VMEM((var, 8, width), f32),
            pltpu.VMEM((8, width), f32),
            dma((cols + 1,)), dma((var,)), dma((var,)), dma,
            dma((samp, var)), dma((samp, var)), dma((var,)), dma((var,)),
            dma((samp, var)), dma((samp, var)), dma((samp, var)), dma((samp, var)),
            dma((2, var)), dma((2, var)), dma((samp,)), dma((samp,)), dma((var,)), dma((var,)),
        ],
        compiler_params=pltpu.CompilerParams(collective_id=0, has_side_effects=True),
        name="columns",
    )(near_idx, wanted, own_slot, want, observed, blocks, diagonal.reshape(cols, 1, width))

    group = 4
    new_blocks, new_diagonal, objective = pl.pallas_call(
        functools.partial(unpack_kernel, group, float(cols * width * var)),
        out_shape=(
            jax.ShapeDtypeStruct(blocks.shape, jnp.float32),
            jax.ShapeDtypeStruct((cols, width), jnp.float32),
            jax.ShapeDtypeStruct((STEPS,), jnp.float32),
        ),
        grid=(cols // group,),
        in_specs=[smem, smem, smem, vmem, vmem, vmem],
        out_specs=(
            pl.BlockSpec((group, 2, width, width), lambda g: (g, 0, 0, 0)),
            pl.BlockSpec((cols, width), lambda g: (0, 0)),
            smem,
        ),
        name="unpack",
    )(owner, rank, diag_slot, fin, tails, whole)
    return new_blocks, new_diagonal.reshape(-1), objective


def advance(diag_block, off_block, diag_values, grad_diag, grad_off, diag_mask, total_rows):
    grad_diag = grad_diag / total_rows
    grad_off = grad_off / total_rows
    new_off = shrink(off_block - step_length * grad_off, step_length * penalty)
    new_diag_block = jnp.where(
        diag_mask, 0.0, shrink(diag_block - step_length * grad_diag, step_length * penalty)
    )
    along = jnp.sum(jnp.where(diag_mask, grad_diag, 0.0), axis=1)
    moved = diag_values - step_length * along
    new_values = 0.5 * (moved + jnp.sqrt(moved * moved + 4.0 * step_length))
    return (new_diag_block, new_off, new_values)


def body(observed, blocks, diagonal, pattern):
    col_count = blocks.shape[0]
    block_width = blocks.shape[2]
    sample_rows = observed.shape[0]
    var_count = lax.axis_size("var")
    samp_count = lax.axis_size("samp")
    capacity = max(2, -(-col_count // var_count))
    total_rows = sample_rows * samp_count
    matrix_order = col_count * block_width * var_count
    var_index = lax.axis_index("var")
    column_ids = jnp.arange(col_count, dtype=jnp.int32)
    columns = var_index * col_count + column_ids
    on_diag = pattern == columns[:, None]
    off_row = jnp.sum(jnp.where(on_diag, 0, pattern), axis=1)
    owner_index = off_row // col_count
    resident_block = off_row % col_count
    earlier = (owner_index[None, :] == owner_index[:, None]) & (
        column_ids[None, :] < column_ids[:, None]
    )
    position_rank = jnp.sum(earlier, axis=1)
    slot_index = owner_index * capacity + position_rank
    all_slots = jnp.arange(var_count * capacity, dtype=jnp.int32)
    slot_match = slot_index[:, None] == all_slots[None, :]
    wanted = jnp.sum(jnp.where(slot_match, resident_block[:, None], 0), axis=0)
    asked_blocks = lax.all_to_all(wanted, "var", split_axis=0, concat_axis=0, tiled=True)
    nearby_panels = observed.reshape(sample_rows, col_count, block_width)
    outgoing = jnp.take(nearby_panels, asked_blocks, axis=1)
    arrived = lax.all_to_all(outgoing, "var", split_axis=1, concat_axis=1, tiled=True)
    distant_panels = jnp.take(arrived, slot_index, axis=1)
    diag_mask = jnp.eye(block_width, dtype=bool)
    flags = on_diag[:, :, None, None]
    diag_block = jnp.sum(jnp.where(flags, blocks, 0.0), axis=1)
    diag_block = jnp.where(diag_mask, 0.0, diag_block)
    off_block = jnp.sum(jnp.where(flags, 0.0, blocks), axis=1)
    diag_values = diagonal.reshape(col_count, block_width)
    samp_first = (lax.axis_index("samp") == 0).astype(jnp.float32)
    objective_parts = []
    for iteration in range(STEPS):
        full_diag = jnp.where(diag_mask, diag_values[:, None, :], diag_block)
        product = jnp.einsum(
            "qlh,lhy->qly",
            nearby_panels,
            full_diag.astype(jnp.bfloat16),
            preferred_element_type=jnp.float32,
        )
        product = product + jnp.einsum(
            "qlh,lhy->qly",
            distant_panels,
            off_block.astype(jnp.bfloat16),
            preferred_element_type=jnp.float32,
        )
        squares = jnp.sum(product * product)
        local_terms = -jnp.sum(jnp.log(diag_values)) + penalty * (
            jnp.sum(jnp.abs(diag_block)) + jnp.sum(jnp.abs(off_block))
        )
        part_value = (squares / (2.0 * total_rows) + samp_first * local_terms) / matrix_order
        objective_parts.append(part_value)
        lower_precision_product = product.astype(jnp.bfloat16)
        grad_diag = jnp.einsum(
            "rei,reo->eio",
            nearby_panels,
            lower_precision_product,
            preferred_element_type=jnp.float32,
        )
        grad_off = jnp.einsum(
            "rei,reo->eio",
            distant_panels,
            lower_precision_product,
            preferred_element_type=jnp.float32,
        )
        grad_diag, grad_off = lax.psum((grad_diag, grad_off), "samp")
        diag_block, off_block, diag_values = advance(
            diag_block, off_block, diag_values, grad_diag, grad_off, diag_mask, total_rows
        )
    objective = lax.psum(jnp.stack(objective_parts), ("samp", "var"))
    new_blocks = jnp.where(flags, diag_block[:, None], off_block[:, None])
    return (new_blocks, diag_values.reshape(-1), objective)


def power_of_two(count):
    return count & (count - 1) == 0


def whole_body(observed, blocks, diagonal, pattern):
    cols = blocks.shape[0]
    var, samp = lax.axis_size("var"), lax.axis_size("samp")
    exact = samp == 4 and samp * var == cols and cols % 4 == 0 and var % 8 == 0 and blocks.shape[2] == 128
    if exact and power_of_two(samp) and power_of_two(var):
        return column_body(observed, blocks, diagonal, pattern)
    return body(observed, blocks, diagonal, pattern)


def solution(mesh):
    placed = (P("samp", "var"), P("var", None, None, None), P("var"), P("var", None))
    return jax.shard_map(
        whole_body,
        mesh=mesh,
        in_specs=placed,
        out_specs=(P("var", None, None, None), P("var"), P()),
        check_vma=False,
    )
```
